256 devices in a mesh: space: 64 (over z, x, core), rep: 4 (over y).
Axes of the slice: x: 4, y: 4, z: 8, core: 2. Of those that a mesh axis runs over, the one named last changes fastest.
Arguments:
- features: bfloat16 [4, 32768, 256], P('rep', 'space'), may hold values from -6 to 6
- neighbours: int32 [4, 32768, 27], P('rep', 'space'), may hold values from -1 to 32767, as said below
- serial: int32 [4, 32768], P('rep', 'space'), may hold values from 0 to 32767, as said below
- w_conv: bfloat16 [6912, 256], replicated, may hold values from -0.078125 to 0.078125
- w_qkv: bfloat16 [256, 768], replicated, may hold values from -45 to 45
- w_proj: bfloat16 [256, 256], replicated, may hold values from -0.375 to 0.375
- cotangent: bfloat16 [4, 32768, 256], P('rep', 'space'), may hold values from -6 to 6
Outputs:
- output: bfloat16 [4, 32768, 256], P('rep', 'space')
- g_conv: float32 [6912, 256], P('space')
- g_qkv: float32 [256, 768], P('space')
- g_proj: float32 [256, 256], P('space')
The draws below stay inside these ranges and needn't reach their ends.
Inputs may be any that keep to these rules, and one draw needn't show every extreme that they name: `neighbours`: entry k of a voxel's row names the row (within its window, slab after slab of 512 rows) of its neighbour at the k-th of 27 offsets, or -1 where there is none; entry 13 is the voxel itself. A neighbour lies in the voxel's own slab, in the last 128 rows of the slab below, or in the first 128 rows of the slab above. `serial`: each window's row is a permutation. The voxels of one slab take at most 16 of the positions of one aligned block of 512 serialized positions, and every slab takes exactly 16 in some block.
All inputs are finite; a program needn't handle non-finite values.
Results may differ from the reference program's by a relative error of at most 0.02.
The reference program's roundings to bfloat16 on the way count: a program that leaves them out, or rounds other values in their place, can miss the bound.
Values may be sent and summed in bfloat16 or wider, within the bound.
No kernel may reach another device: no remote copies, remote signals or barrier semaphores. Data moves between devices by JAX's collectives and lax.ppermute only.
A program may use at most 64 MiB of HBM per device.

```python
import jax
import jax.numpy as jnp
from jax import lax

C = 256
HEADS = 8
PATCH = 512
V = 512
RIM = 128
NPTS = 32768
REPS = 4


def draw_neighbours(key, part):
    keys = jax.random.split(key, 3)
    slab_count = NPTS // V
    shape = (REPS, NPTS, 27)
    row_ids = jnp.arange(NPTS, dtype=jnp.int32)[None, :, None]
    slab_ids = row_ids // V
    inside = row_ids % V
    offsets = jnp.arange(27, dtype=jnp.int32)[None, None, :]
    jitter = jax.random.randint(keys[0], shape, -64, 65)
    nearby = jnp.clip(inside + jitter, 0, V - 1) + slab_ids * V
    picked = jax.random.randint(keys[1], shape, 0, RIM)
    lower = (offsets < 9) & (inside < RIM) & (slab_ids > 0)
    upper = (offsets >= 18) & (inside >= V - RIM) & (slab_ids < slab_count - 1)
    below = (slab_ids - 1) * V + V - RIM + picked
    above = (slab_ids + 1) * V + picked
    target = jnp.where(lower, below, jnp.where(upper, above, nearby))
    alive = jax.random.randint(keys[2], shape, 0, 10) < 6
    target = jnp.where(alive, target, -1)
    target = jnp.where(offsets == 13, row_ids, target)
    return target.astype(jnp.int32)


def serial_window(key):
    slab_count = NPTS // V
    share = V // slab_count
    keys = jax.random.split(key, 4)
    amounts = jax.random.randint(keys[0], (slab_count // 2,), 0, share + 1).at[0].set(share)
    order = jax.random.permutation(keys[1], slab_count)
    signed = jnp.concatenate([amounts, -amounts]).astype(jnp.int32)
    shifts = jnp.zeros((slab_count,), jnp.int32).at[order].set(signed)
    owner_ids = jnp.arange(slab_count, dtype=jnp.int32)
    counts = share + shifts[(owner_ids[:, None] - owner_ids[None, :]) % slab_count]
    inclusive = jnp.cumsum(counts, axis=0)
    exclusive = inclusive - counts
    earlier = jnp.cumsum(counts, axis=1) - counts
    ranking = jax.vmap(lambda subkey: jax.random.permutation(subkey, V))(jax.random.split(keys[2], slab_count)).astype(jnp.int32)
    owners = jnp.sum((inclusive.T[:, None, :] <= ranking[:, :, None]).astype(jnp.int32), axis=-1)
    slab_col = owner_ids[:, None]
    within = ranking - exclusive[owners, slab_col] + earlier[owners, slab_col]
    shuffle = jax.vmap(lambda subkey: jax.random.permutation(subkey, V))(jax.random.split(keys[3], slab_count)).astype(jnp.int32)
    position = owners * V + shuffle[owners, within]
    return position.reshape(NPTS).astype(jnp.int32)


def draw_serial(key, part):
    return jax.vmap(serial_window)(jax.random.split(key, REPS))


def draw_w_qkv(key, part):
    keys = jax.random.split(key, 1)
    base = jnp.clip(jax.random.normal(keys[0], (C, 3 * C), jnp.float32), -6.0, 6.0) / C ** 0.5
    return base.astype(jnp.bfloat16)


def levels(stream_key, shape, cuts, smallest, largest):
    level, own = 1.0, jax.random.fold_in(stream_key, 6)
    for axis_at, parts in cuts:
        draws = jnp.exp(jax.random.uniform(jax.random.fold_in(own, axis_at), (parts,), jnp.float32, smallest / len(cuts), largest / len(cuts)))
        level = level * jnp.repeat(draws, shape[axis_at] // parts).reshape([-1 if axis == axis_at else 1 for axis in range(len(shape))])
    return level


def bell_draw(key, dims, spread, limit, cuts=(), held_as=jnp.bfloat16):
    drawn = jax.random.normal(key, dims, jnp.float32) * spread
    if len(cuts) > 0:
        drawn = levels(key, dims, cuts, -0.22, 0.18) * drawn
    return jnp.clip(drawn, min=-limit, max=limit).astype(held_as)


def setup_inputs(seed: int = 0) -> dict:
    key_list = jax.random.split(jax.random.key(seed), 8)
    features = bell_draw(key_list[0], (REPS, NPTS, C), 1.0, 6.0, ((0, 4), (1, 64)))
    neighbours = draw_neighbours(jax.random.fold_in(key_list[7], 71), 0)
    serial = draw_serial(jax.random.fold_in(key_list[7], 71), 0)
    w_conv = bell_draw(key_list[3], (27 * C, C), (27 * C) ** -0.5, 0.078125)
    w_qkv = draw_w_qkv(jax.random.fold_in(key_list[7], 71), 0)
    w_proj = bell_draw(key_list[5], (C, C), C ** -0.5, 0.375)
    cotangent = bell_draw(key_list[6], (REPS, NPTS, C), 1.0, 6.0, ((0, 4), (1, 64)))
    return dict(features=features, neighbours=neighbours, serial=serial, w_conv=w_conv, w_qkv=w_qkv, w_proj=w_proj, cotangent=cotangent)


EPSILON = 1e-05

def norm_rows(patched):
    values = patched.astype(jnp.float32)
    centre = values - lax.optimization_barrier(jnp.mean(values, axis=-1, keepdims=True))
    inverse = lax.rsqrt(lax.optimization_barrier(jnp.mean(centre * centre, axis=-1, keepdims=True)) + EPSILON)
    return (centre * inverse, inverse)

def split_heads(block):
    length, channels = block.shape
    return block.reshape(length // PATCH, PATCH, HEADS, channels // HEADS).transpose(0, 2, 1, 3).reshape(-1, PATCH, channels // HEADS)

def merge_heads(block, length):
    items, patch_len, depth = block.shape
    return block.reshape(length // patch_len, HEADS, patch_len, depth).transpose(0, 2, 1, 3).reshape(length, HEADS * depth)

def head_probability(queries, key_rows):
    scores = jnp.einsum('qd,kd->qk', queries.astype(jnp.float32), key_rows.astype(jnp.float32))
    exponent = jnp.exp(scores - lax.optimization_barrier(jnp.max(scores, axis=1, keepdims=True)))
    return exponent / lax.optimization_barrier(jnp.sum(exponent, axis=1, keepdims=True))

def head_forward(item):
    queries, key_rows, value_rows = item
    weights = head_probability(queries, key_rows).astype(jnp.bfloat16)
    return jnp.einsum('qk,kd->qd', weights.astype(jnp.float32), value_rows.astype(jnp.float32)).astype(jnp.bfloat16)

def head_backward(item):
    queries, key_rows, value_rows, d_out = item
    weights = head_probability(queries, key_rows)
    rounded = weights.astype(jnp.bfloat16).astype(jnp.float32)
    d_out32 = d_out.astype(jnp.float32)
    d_value = jnp.einsum('qk,qd->kd', rounded, d_out32)
    d_prob = jnp.einsum('qd,kd->qk', d_out32, value_rows.astype(jnp.float32))
    d_scores = (weights * (d_prob - lax.optimization_barrier(jnp.sum(d_prob * weights, axis=1, keepdims=True)))).astype(jnp.bfloat16).astype(jnp.float32)
    d_query = jnp.einsum('qk,kd->qd', d_scores, key_rows.astype(jnp.float32))
    d_key = jnp.einsum('qk,qd->kd', d_scores, queries.astype(jnp.float32))
    return (d_query, d_key, d_value)

def one_window(features, neighbours, serial, w_conv, w_qkv, w_proj, cotangent):
    length, channels = features.shape
    factor = (channels // HEADS) ** (-0.5)
    padded = jnp.concatenate([features, jnp.zeros((1, channels), jnp.bfloat16)], 0)
    linked = jnp.where(neighbours < 0, length, neighbours).astype(jnp.int32)
    blocks = linked.reshape(length // V, V, 27)

    def conv_block(block):
        gathered = padded[block].reshape(V, 27 * channels)
        return jnp.dot(gathered, w_conv, preferred_element_type=jnp.float32)
    conv = lax.map(conv_block, blocks).reshape(length, channels)
    mixed = (features.astype(jnp.float32) + conv).astype(jnp.bfloat16)
    patched = jnp.zeros_like(mixed).at[serial].set(mixed)
    centred, inverse = norm_rows(patched)
    normed = centred.astype(jnp.bfloat16)
    qkv = jnp.dot(normed, w_qkv, preferred_element_type=jnp.float32)
    queries = (qkv[:, :channels] * factor).astype(jnp.bfloat16)
    key_rows = qkv[:, channels:2 * channels].astype(jnp.bfloat16)
    value_rows = qkv[:, 2 * channels:].astype(jnp.bfloat16)
    items = (split_heads(queries), split_heads(key_rows), split_heads(value_rows))
    attended = merge_heads(lax.map(head_forward, items), length)
    out_patch = (patched.astype(jnp.float32) + jnp.dot(attended, w_proj, preferred_element_type=jnp.float32)).astype(jnp.bfloat16)
    output = out_patch[serial]
    upstream = jnp.zeros_like(cotangent).at[serial].set(cotangent)
    g_proj = jnp.dot(attended.T, upstream, preferred_element_type=jnp.float32)
    d_att = jnp.dot(upstream, w_proj.T, preferred_element_type=jnp.float32).astype(jnp.bfloat16)
    d_query, d_key, d_value = lax.map(head_backward, items + (split_heads(d_att),))
    d_qkv = jnp.concatenate([merge_heads(d_query, length) * factor, merge_heads(d_key, length), merge_heads(d_value, length)], 1).astype(jnp.bfloat16)
    g_qkv = jnp.dot(normed.T, d_qkv, preferred_element_type=jnp.float32)
    d_norm = jnp.dot(d_qkv, w_qkv.T, preferred_element_type=jnp.float32)
    d_layer = inverse * (d_norm - lax.optimization_barrier(jnp.mean(d_norm, axis=-1, keepdims=True)) - centred * lax.optimization_barrier(jnp.mean(d_norm * centred, axis=-1, keepdims=True)))
    d_patch = (upstream.astype(jnp.float32) + d_layer).astype(jnp.bfloat16)
    d_mixed = d_patch[serial]

    def conv_grad(total, pair):
        block, grads = pair
        gathered = padded[block].reshape(V, 27 * channels)
        return (total + jnp.dot(gathered.T, grads, preferred_element_type=jnp.float32), None)
    g_conv = lax.scan(conv_grad, jnp.zeros((27 * channels, channels), jnp.float32), (blocks, d_mixed.reshape(length // V, V, channels)))[0]
    return (output, g_conv, g_qkv, g_proj)

def reference(features, neighbours, serial, w_conv, w_qkv, w_proj, cotangent):
    outputs = []
    g_conv = jnp.zeros((27 * C, C), jnp.float32)
    g_qkv = jnp.zeros((C, 3 * C), jnp.float32)
    g_proj = jnp.zeros((C, C), jnp.float32)
    for window in range(REPS):
        result = one_window(features[window], neighbours[window], serial[window], w_conv, w_qkv, w_proj, cotangent[window])
        outputs.append(result[0])
        g_conv = g_conv + result[1]
        g_qkv = g_qkv + result[2]
        g_proj = g_proj + result[3]
    return (jnp.stack(outputs, 0), g_conv, g_qkv, g_proj)
```

```python
import functools

import jax
import jax.numpy as jnp
from jax import lax
from jax.experimental import pallas as pl
from jax.experimental.pallas import tpu as pltpu
from jax.sharding import Mesh
from jax.sharding import PartitionSpec as P

HEADS = 8
RIM = 128
EPSILON = 1e-05
SPACE = ("z", "x", "c")
VACANT = 512.0
OFFSETS_PER_STEP = 3

F32 = jnp.float32
BF16 = jnp.bfloat16


def iota(shape, dim):
    return lax.broadcasted_iota(jnp.int32, shape, dim)


def mm(a, b):
    return jnp.dot(a, b, preferred_element_type=F32)


def mm_nt(a, b):
    return lax.dot_general(a, b, (((1,), (1,)), ((), ())), preferred_element_type=F32)


def mm_tn(a, b):
    return lax.dot_general(a, b, (((0,), (0,)), ((), ())), preferred_element_type=F32)


def one_hot(mask):
    return jnp.where(mask, 1.0, 0.0).astype(BF16)


def turned(a):
    return jnp.transpose(a.astype(F32), (1, 0))


def cost(flops, nbytes):
    return pl.CostEstimate(flops=int(flops), bytes_accessed=int(nbytes), transcendentals=0)


VMEM_SPEC = pl.BlockSpec(memory_space=pltpu.VMEM)


def pack_kernel(capacity, serial_ref, cot_ref, buf_ref, slot_ref):
    length, channels = cot_ref.shape
    slots = buf_ref.shape[0]
    owners = slots // capacity
    owner = lax.div(serial_ref[...], jnp.int32(length))
    member = iota((owners, length), 0) == owner
    before = one_hot(iota((length, length), 0) < iota((length, length), 1))
    earlier = mm(one_hot(member), before)
    place = earlier + (capacity * iota((owners, length), 0)).astype(F32)
    slot = jnp.sum(jnp.where(member, place, 0.0), axis=0, keepdims=True)
    slot_ref[...] = jnp.broadcast_to(slot, slot_ref.shape)
    mask = iota((slots, length), 0) == slot.astype(jnp.int32)
    pick = one_hot(mask)
    taken = jnp.sum(jnp.where(mask, 1.0, 0.0), axis=1, keepdims=True)
    vacant = jnp.where(taken > 0.5, 0.0, VACANT)
    buf_ref[...] = (mm(pick, cot_ref[...]) + vacant).astype(BF16)


def pack_cot(serial, cot, slots, capacity):
    length, channels = cot.shape
    return pl.pallas_call(
        functools.partial(pack_kernel, capacity),
        out_shape=(
            jax.ShapeDtypeStruct((slots, channels), BF16),
            jax.ShapeDtypeStruct((8, length), F32),
        ),
        in_specs=[VMEM_SPEC] * 2,
        out_specs=(VMEM_SPEC, VMEM_SPEC),
        cost_estimate=cost(2 * slots * length * channels, 2 << 20),
        name="pack_cot",
    )(serial, cot)


def conv_kernel(nb_ref, below_ref, own_ref, above_ref, w_ref, slot_ref, g_ref, buf_ref, table, acc):
    step = pl.program_id(0)
    length, channels = own_ref.shape
    slots = buf_ref.shape[0]
    rows = table.shape[1]
    index = (lax.axis_index("z") * lax.axis_size("x") + lax.axis_index("x")) * lax.axis_size(
        "c"
    ) + lax.axis_index("c")
    base = index * length - RIM

    @pl.when(step == 0)
    def _():
        table[:, :RIM] = turned(below_ref[...]).astype(BF16)
        table[:, RIM : RIM + length] = turned(own_ref[...]).astype(BF16)
        table[:, RIM + length :] = turned(above_ref[...]).astype(BF16)
        acc[...] = jnp.zeros_like(acc)

    total = acc[...]
    for j in range(nb_ref.shape[0]):
        linked = nb_ref[j]
        local = jnp.where(linked < 0, -1, linked - base)
        pick = one_hot(iota((rows, length), 0) == local)
        gathered = mm(table[...], pick).astype(BF16)
        g_ref[j * channels : (j + 1) * channels, :] = gathered
        total = total + mm_tn(w_ref[j * channels : (j + 1) * channels, :], gathered)
    acc[...] = total

    @pl.when(step == pl.num_programs(0) - 1)
    def _():
        mixed = (own_ref[...].astype(F32) + turned(acc[...])).astype(BF16)
        pick = one_hot(iota((slots, length), 0) == slot_ref[0:1, :].astype(jnp.int32))
        buf_ref[...] = mm(pick, mixed).astype(BF16)


def gather_conv(nb, below, own, above, w_conv, slot, slots):
    length, channels = own.shape
    count = nb.shape[0]
    per = OFFSETS_PER_STEP
    rows = length + 2 * RIM
    whole = lambda *shape: pl.BlockSpec(shape, lambda i: (0,) * len(shape))
    return pl.pallas_call(
        conv_kernel,
        grid=(count // per,),
        out_shape=(
            jax.ShapeDtypeStruct((count * channels, length), BF16),
            jax.ShapeDtypeStruct((slots, channels), BF16),
        ),
        in_specs=[
            pl.BlockSpec((per, 1, length), lambda i: (i, 0, 0)),
            whole(RIM, channels),
            whole(length, channels),
            whole(RIM, channels),
            pl.BlockSpec((per * channels, channels), lambda i: (i, 0)),
            whole(8, length),
        ],
        out_specs=(
            pl.BlockSpec((per * channels, length), lambda i: (i, 0)),
            whole(slots, channels),
        ),
        scratch_shapes=[pltpu.VMEM((channels, rows), BF16), pltpu.VMEM((channels, length), F32)],
        compiler_params=pltpu.CompilerParams(dimension_semantics=("arbitrary",)),
        cost_estimate=cost(2 * count * length * channels * (rows + channels), 12 << 20),
        name="gather_conv",
    )(nb, below, own, above, w_conv, slot)


def arrive_kernel(cot_ref, w_ref, up_ref, datt_ref, datt_t_ref, row_ref, col_ref):
    slots, channels = cot_ref.shape
    length = up_ref.shape[0]
    arrived = cot_ref[...]
    valid = jnp.broadcast_to(arrived[:, 0:1].astype(F32), (slots, 128)) < VACANT / 2
    lower = one_hot(iota((slots, slots), 1) < iota((slots, slots), 0))
    ahead = mm(lower, one_hot(valid))
    col = jnp.where(valid, ahead, -1.0)
    col_ref[...] = col
    row = jnp.transpose(col, (1, 0))[0:8, :]
    row_ref[...] = row
    pick = one_hot(iota((length, slots), 0) == row[0:1, :].astype(jnp.int32))
    upstream = mm(pick, arrived).astype(BF16)
    up_ref[...] = upstream
    d_att = mm_nt(upstream, w_ref[...]).astype(BF16)
    datt_ref[...] = d_att
    datt_t_ref[...] = turned(d_att).astype(BF16)


def arrive(cot_buf, w_proj, length):
    slots, channels = cot_buf.shape
    return pl.pallas_call(
        arrive_kernel,
        out_shape=(
            jax.ShapeDtypeStruct((length, channels), BF16),
            jax.ShapeDtypeStruct((length, channels), BF16),
            jax.ShapeDtypeStruct((channels, length), BF16),
            jax.ShapeDtypeStruct((8, slots), F32),
            jax.ShapeDtypeStruct((slots, 128), F32),
        ),
        in_specs=[VMEM_SPEC] * 2,
        out_specs=(VMEM_SPEC,) * 5,
        cost_estimate=cost(2 * slots * length * channels * 3, 2 << 20),
        name="arrive",
    )(cot_buf, w_proj)


def patch_kernel(
    mix_ref,
    up_ref,
    datt_ref,
    datt_t_ref,
    row_ref,
    col_ref,
    wqkv_ref,
    wproj_ref,
    out_ref,
    dp_ref,
    gw_ref,
    att_t,
    dq_t,
    dk,
    dv,
):
    length, channels = up_ref.shape
    slots = mix_ref.shape[0]
    depth = channels // HEADS
    factor = depth ** (-0.5)
    group = 128
    pick = one_hot(iota((length, slots), 0) == row_ref[0:1, :].astype(jnp.int32))
    patched = mm(pick, mix_ref[...])
    values_t = turned(patched)
    centre_t = values_t - jnp.mean(values_t, axis=0, keepdims=True)
    inverse = lax.rsqrt(jnp.mean(centre_t * centre_t, axis=0, keepdims=True) + EPSILON)
    centred_t = centre_t * inverse
    normed_t = centred_t.astype(BF16)
    w_qkv = wqkv_ref[...]
    qkv_t = mm_tn(w_qkv, normed_t)
    q_t = (qkv_t[:channels] * factor).astype(BF16)
    k_t = qkv_t[channels : 2 * channels].astype(BF16)
    v_t = qkv_t[2 * channels :].astype(BF16)
    q = turned(q_t).astype(BF16)
    k = turned(k_t).astype(BF16)
    v = turned(v_t).astype(BF16)
    d_att = datt_ref[...]
    d_att_t = datt_t_ref[...]
    lane = iota((length, group), 1)
    sub = iota((group, length), 0)
    zero = jnp.zeros((), BF16)
    for g in range(channels // group):
        span = slice(g * group, (g + 1) * group)
        k_g, v_g = k[:, span], v[:, span]
        q_g, da_g = q[:, span], d_att[:, span]
        q_tg, da_tg = q_t[span], d_att_t[span]
        dk_g = jnp.zeros((length, group), F32)
        dv_g = jnp.zeros((length, group), F32)
        for h in range(group // depth):
            in_rows = lax.div(sub, jnp.int32(depth)) == h
            in_lanes = lax.div(lane, jnp.int32(depth)) == h
            at = g * group + h * depth
            scores = mm(k_g, jnp.where(in_rows, q_tg, zero))
            e = jnp.exp(scores - jnp.max(scores, axis=0, keepdims=True))
            p = e * (1.0 / jnp.sum(e, axis=0, keepdims=True))
            pb = p.astype(BF16)
            att_t[at : at + depth, :] = mm(v_t[at : at + depth], pb)
            dv_g = dv_g + mm(pb, jnp.where(in_lanes, da_g, zero))
            dp = mm(v_g, jnp.where(in_rows, da_tg, zero))
            ds = (p * (dp - jnp.sum(dp * p, axis=0, keepdims=True))).astype(BF16)
            dq_t[at : at + depth, :] = mm(k_t[at : at + depth], ds)
            dk_g = dk_g + mm(ds, jnp.where(in_lanes, q_g, zero))
        dk[:, span] = dk_g
        dv[:, span] = dv_g
    attended_t = att_t[...].astype(BF16)
    attended = turned(attended_t).astype(BF16)
    out_patch = (patched + mm(attended, wproj_ref[...])).astype(BF16)
    upstream = up_ref[...]
    gw_ref[:, 3 * channels :] = mm(attended_t, upstream)
    dq_t_full = dq_t[...] * factor
    dk_full, dv_full = dk[...], dv[...]
    gw_ref[:, :channels] = mm(normed_t, turned(dq_t_full).astype(BF16))
    gw_ref[:, channels : 2 * channels] = mm(normed_t, dk_full.astype(BF16))
    gw_ref[:, 2 * channels : 3 * channels] = mm(normed_t, dv_full.astype(BF16))
    d_norm = mm(w_qkv[:, :channels], dq_t_full.astype(BF16))
    d_norm = d_norm + mm(w_qkv[:, channels : 2 * channels], turned(dk_full).astype(BF16))
    d_norm = d_norm + mm(w_qkv[:, 2 * channels :], turned(dv_full).astype(BF16))
    d_layer = inverse * (
        d_norm
        - jnp.mean(d_norm, axis=0, keepdims=True)
        - centred_t * jnp.mean(d_norm * centred_t, axis=0, keepdims=True)
    )
    d_patch = (upstream.astype(F32) + turned(d_layer)).astype(BF16)
    key = jnp.broadcast_to(col_ref[:, 0:1].astype(jnp.int32), (slots, length))
    back = one_hot(iota((slots, length), 1) == key)
    dp_ref[...] = mm(back, d_patch).astype(BF16)
    out_ref[...] = mm(back, out_patch).astype(BF16)


def patch(mix_buf, up, d_att, d_att_t, row, col, w_qkv, w_proj):
    slots, channels = mix_buf.shape
    length = up.shape[0]
    return pl.pallas_call(
        patch_kernel,
        out_shape=(
            jax.ShapeDtypeStruct((slots, channels), BF16),
            jax.ShapeDtypeStruct((slots, channels), BF16),
            jax.ShapeDtypeStruct((channels, 4 * channels), F32),
        ),
        in_specs=[VMEM_SPEC] * 8,
        out_specs=(VMEM_SPEC,) * 3,
        scratch_shapes=[
            pltpu.VMEM((channels, length), F32),
            pltpu.VMEM((channels, length), F32),
            pltpu.VMEM((length, channels), F32),
            pltpu.VMEM((length, channels), F32),
        ],
        cost_estimate=cost(14e9, 4 << 20),
        name="patch",
    )(mix_buf, up, d_att, d_att_t, row, col, w_qkv, w_proj)


def unpack(slot, buf):
    slots = buf.shape[0]
    length = slot.shape[1]
    wide = jnp.transpose(jnp.broadcast_to(slot[0:1, :], (128, length)), (1, 0))
    key = jnp.broadcast_to(wide[:, 0:1].astype(jnp.int32), (length, slots))
    return mm(one_hot(iota((length, slots), 1) == key), buf).astype(BF16)


def output_kernel(slot_ref, buf_ref, out_ref):
    out_ref[...] = unpack(slot_ref[...], buf_ref[...])


def return_rows(slot, buf):
    length, channels = slot.shape[1], buf.shape[1]
    return pl.pallas_call(
        output_kernel,
        out_shape=jax.ShapeDtypeStruct((length, channels), BF16),
        in_specs=[VMEM_SPEC] * 2,
        out_specs=VMEM_SPEC,
        cost_estimate=cost(2 * length * buf.shape[0] * channels, 1 << 20),
        name="return_rows",
    )(slot, buf)


PIECE = 128
PART = 16


def grad_kernel(sizes, slot_ref, buf_ref, g_ref, gw_ref, keep_ref, send_ref, d_mixed, total):
    step = pl.program_id(0)
    nz, nx, nc, nrep = sizes
    block = g_ref.shape[0]
    channels = buf_ref.shape[1]

    @pl.when(step == 0)
    def _():
        d_mixed[...] = unpack(slot_ref[...], buf_ref[...])

    total[pl.ds(pl.multiple_of(step * block, block), block), :] = mm(g_ref[...], d_mixed[...])

    @pl.when(step == pl.num_programs(0) - 1)
    def _():
        full = block * pl.num_programs(0)
        mine = (lax.axis_index("z"), lax.axis_index("x"), lax.axis_index("c"), lax.axis_index("rep"))
        rows = total.shape[0] // (nz * nx * nc)
        fine = gw_ref.shape[0] // (nz * nx * nc)
        for core in range(nc):
            for is_mine, ref in ((True, keep_ref), (False, send_ref)):
                same = mine[2] == core

                @pl.when(same if is_mine else jnp.logical_not(same))
                def _(core=core, ref=ref):
                    for z in range(nz):
                        sz = lax.rem(z - mine[0] + nz, nz)
                        for x in range(nx):
                            sx = lax.rem(x - mine[1] + nx, nx)
                            d = (z * nx + x) * nc + core
                            for part in range(PIECE // PART):
                                half, y = part // nrep, part % nrep
                                sy = lax.rem(y - mine[3] + nrep, nrep)
                                first = part * PART
                                if part == PIECE // PART - 1:
                                    terms = [
                                        gw_ref[
                                            d * fine : (d + 1) * fine,
                                            j * channels : (j + 1) * channels,
                                        ]
                                        for j in range(4)
                                    ]
                                    value = jnp.concatenate(terms, axis=0)
                                elif first + PART <= rows:
                                    value = total[d * rows + first : d * rows + first + PART, :]
                                else:
                                    left = rows - first
                                    value = jnp.concatenate(
                                        [
                                            total[d * rows + first : d * rows + rows, :],
                                            jnp.zeros((PART - left, channels), F32),
                                        ],
                                        axis=0,
                                    )
                                lead = sx * nrep + sy if half == 0 else sy * nx + sx
                                ref[half, lead, sz] = value.astype(BF16)


def grad_terms(slot, buf, g, gw, sizes):
    slots, channels = buf.shape
    length = slot.shape[1]
    nz, nx, nc, nrep = sizes
    block = 3 * channels
    whole = lambda *shape: pl.BlockSpec(shape, lambda i: (0,) * len(shape))
    shape = (2, nx * nrep, nz, PART, channels)
    return pl.pallas_call(
        functools.partial(grad_kernel, sizes),
        grid=(g.shape[0] // block,),
        out_shape=(jax.ShapeDtypeStruct(shape, BF16), jax.ShapeDtypeStruct(shape, BF16)),
        in_specs=[
            whole(8, length),
            whole(slots, channels),
            pl.BlockSpec((block, length), lambda i: (i, 0)),
            whole(*gw.shape),
        ],
        out_specs=(whole(*shape), whole(*shape)),
        scratch_shapes=[
            pltpu.VMEM((length, channels), BF16),
            pltpu.VMEM((g.shape[0], channels), F32),
        ],
        compiler_params=pltpu.CompilerParams(dimension_semantics=("arbitrary",)),
        cost_estimate=cost(2 * g.shape[0] * length * channels, 12 << 20),
        name="grad_terms",
    )(slot, buf, g, gw)


def add_kernel(plan, *refs):
    count = sum(len(sources) for sources, _ in plan)
    ins, outs = refs[:count], refs[count:]
    at, to = 0, 0
    for sources, parts in plan:
        group = ins[at : at + len(sources)]
        at += len(sources)
        for part in range(parts):
            value = None
            for ref, (lead, per) in zip(group, sources):
                term = ref[lead + part * per : lead + (part + 1) * per].astype(F32)
                value = term if value is None else value + term
            outs[to][...] = value.astype(BF16)
            to += 1


def add_up(terms):
    plan, arrays, shapes = [], [], []
    for sources, lead_rows, parts in terms:
        per = lead_rows // parts
        plan.append((tuple((lead, per) for _, lead in sources), parts))
        arrays += [a for a, _ in sources]
        tail = sources[0][0].shape[1:]
        shapes += [jax.ShapeDtypeStruct((per, *tail), BF16)] * parts
    nbytes = sum(2 * s.size for s in shapes) * 3
    return pl.pallas_call(
        functools.partial(add_kernel, tuple(plan)),
        out_shape=tuple(shapes),
        in_specs=[VMEM_SPEC] * len(arrays),
        out_specs=(VMEM_SPEC,) * len(shapes),
        cost_estimate=cost(nbytes, nbytes),
        name="add_up",
    )(*arrays)


def final_kernel(sizes, *refs):
    nz, nx, nc, nrep = sizes
    ins, (conv_ref, qkv_ref, proj_ref, piece) = refs[:nrep], refs[nrep:]
    me = lax.axis_index("rep")
    rows, channels = conv_ref.shape
    fine = qkv_ref.shape[0]
    for s, ref in enumerate(ins):
        y = lax.rem(me - s + nrep, nrep)
        for half in range(2):
            start = pl.multiple_of((half * nrep + y) * PART, PART)
            piece[pl.ds(start, PART), :] = ref[half * PART : (half + 1) * PART, :].astype(F32)
    conv_ref[...] = piece[:rows, :]
    base = PIECE - PART
    for j in range(3):
        qkv_ref[:, j * channels : (j + 1) * channels] = piece[base + fine * j : base + fine * (j + 1), :]
    proj_ref[...] = piece[base + 3 * fine : base + 4 * fine, :]


def shifted(a, axis, by):
    size = lax.axis_size(axis)
    return lax.ppermute(a, axis, [(i, (i + by) % size) for i in range(size)])


def per_device(features, neighbours, serial, w_conv, w_qkv, w_proj, cotangent):
    feats = features[0]
    length, channels = feats.shape
    slab_count = lax.axis_size(SPACE)
    sizes = tuple(lax.axis_size(a) for a in ("z", "x", "c", "rep"))
    nz, nx, nc, nrep = sizes
    capacity = 2 * length // slab_count
    slots = slab_count * capacity
    up = [(i, i + 1) for i in range(slab_count - 1)]
    down = [(j, i) for i, j in up]

    def exchange(buf):
        parts = buf.reshape(slab_count, capacity, channels)
        out = lax.all_to_all(parts, SPACE, split_axis=0, concat_axis=0, tiled=True)
        return out.reshape(slots, channels)

    below = lax.ppermute(feats[length - RIM :], SPACE, up)
    above = lax.ppermute(feats[:RIM], SPACE, down)
    cot_buf, slot = pack_cot(serial, cotangent[0], slots, capacity)
    cot_in = exchange(cot_buf)
    nb = jnp.transpose(neighbours, (2, 0, 1))
    g, mix_buf = gather_conv(nb, below, feats, above, w_conv, slot, slots)
    mix_in = exchange(mix_buf)
    upstream, d_att, d_att_t, row, col = arrive(cot_in, w_proj, length)
    out_buf, dp_buf, gw = patch(mix_in, upstream, d_att, d_att_t, row, col, w_qkv, w_proj)
    dp_in = exchange(dp_buf)
    out_in = exchange(out_buf)
    output = return_rows(slot, out_in)
    keep, send = grad_terms(slot, dp_in, g, gw, sizes)

    got = lax.ppermute(send, "c", [(0, 1), (1, 0)])
    flat = lambda a: a.reshape(2 * nx * nrep, nz, PART, channels)
    keep, got = flat(keep), flat(got)
    half = nx * nrep
    parts = add_up([([(keep, 0), (got, 0)], half, nx), ([(keep, half), (got, half)], half, nrep)])
    a, b = parts[:nx], parts[nx:]
    a_in = [shifted(a[s], "x", s) for s in range(1, nx)]
    b_in = [shifted(b[s], "rep", s) for s in range(1, nrep)]
    parts = add_up(
        [
            ([(t, 0) for t in [a[0], *a_in]], nrep, nrep),
            ([(t, 0) for t in [b[0], *b_in]], nx, nx),
        ]
    )
    a, b = parts[:nrep], parts[nrep:]
    a_in = [shifted(a[s], "rep", s) for s in range(1, nrep)]
    b_in = [shifted(b[s], "x", s) for s in range(1, nx)]

    def rows_of(t):
        return t.reshape(nz, PART, channels)

    parts = add_up(
        [
            ([(rows_of(t), 0) for t in [a[0], *a_in]], nz, nz),
            ([(rows_of(t), 0) for t in [b[0], *b_in]], nz, nz),
        ]
    )
    ab = [jnp.concatenate([parts[s][0], parts[nz + s][0]], axis=0) for s in range(nz)]
    ab_in = [shifted(ab[s], "z", s) for s in range(1, nz)]
    (own,) = add_up([([(t, 0) for t in [ab[0], *ab_in]], 2 * PART, 1)])
    everyone = [own] + [shifted(own, "rep", s) for s in range(1, nrep)]
    places = slab_count
    g_conv, g_qkv, g_proj = pl.pallas_call(
        functools.partial(final_kernel, sizes),
        out_shape=(
            jax.ShapeDtypeStruct((w_conv.shape[0] // places, channels), F32),
            jax.ShapeDtypeStruct((channels // places, 3 * channels), F32),
            jax.ShapeDtypeStruct((channels // places, channels), F32),
        ),
        in_specs=[VMEM_SPEC] * nrep,
        out_specs=(VMEM_SPEC,) * 3,
        scratch_shapes=[pltpu.VMEM((PIECE, channels), F32)],
        name="final",
    )(*everyone)
    return (output[None], g_conv, g_qkv, g_proj)


def solution(mesh):
    fine = Mesh(mesh.devices.reshape(8, 4, 2, 4), ("z", "x", "c", "rep"))
    return jax.shard_map(
        per_device,
        mesh=fine,
        in_specs=(
            P("rep", SPACE, None),
            P("rep", SPACE, None),
            P("rep", SPACE),
            P(),
            P(),
            P(),
            P("rep", SPACE, None),
        ),
        out_specs=(P("rep", SPACE, None), P(SPACE, None), P(SPACE, None), P(SPACE, None)),
        check_vma=False,
    )
```

```python
import functools

import jax
import jax.numpy as jnp
from jax import lax
from jax.experimental import pallas as pl
from jax.experimental.pallas import tpu as pltpu
from jax.sharding import Mesh
from jax.sharding import PartitionSpec as P


HEADS = 8
RIM = 128
EPSILON = 1e-05
SPACE = ("z", "x", "c")
VACANT = 512.0
OFFSETS_PER_STEP = 3

F32 = jnp.float32
BF16 = jnp.bfloat16


def iota(shape, dim):
    return lax.broadcasted_iota(jnp.int32, shape, dim)


def mm(a, b):
    return jnp.dot(a, b, preferred_element_type=F32)


def mm_nt(a, b):
    return lax.dot_general(a, b, (((1,), (1,)), ((), ())), preferred_element_type=F32)


def mm_tn(a, b):
    return lax.dot_general(a, b, (((0,), (0,)), ((), ())), preferred_element_type=F32)


def one_hot(mask):
    return jnp.where(mask, 1.0, 0.0).astype(BF16)


def turned(a):
    return jnp.transpose(a.astype(F32), (1, 0))


def cost(flops, nbytes):
    return pl.CostEstimate(flops=int(flops), bytes_accessed=int(nbytes), transcendentals=0)


VMEM_SPEC = pl.BlockSpec(memory_space=pltpu.VMEM)


def params(mebibytes, **more):
    return pltpu.CompilerParams(vmem_limit_bytes=mebibytes << 20, **more)


def pack_kernel(capacity, serial_ref, cot_ref, buf_ref, slot_ref):
    length, _ = cot_ref.shape
    slots = buf_ref.shape[0]
    owners = slots // capacity
    owner = lax.div(serial_ref[...], jnp.int32(length))
    member = iota((owners, length), 0) == owner
    before = one_hot(iota((length, length), 0) < iota((length, length), 1))
    earlier = mm(one_hot(member), before)
    place = earlier + (capacity * iota((owners, length), 0)).astype(F32)
    slot = jnp.sum(jnp.where(member, place, 0.0), axis=0, keepdims=True)
    slot_ref[...] = jnp.broadcast_to(slot, slot_ref.shape)
    mask = iota((slots, length), 0) == slot.astype(jnp.int32)
    pick = one_hot(mask)
    taken = jnp.sum(jnp.where(mask, 1.0, 0.0), axis=1, keepdims=True)
    vacant = jnp.where(taken > 0.5, 0.0, VACANT)
    buf_ref[...] = (mm(pick, cot_ref[...]) + vacant).astype(BF16)


def pack_cot(serial, cot, slots, capacity):
    length, channels = cot.shape
    return pl.pallas_call(
        functools.partial(pack_kernel, capacity),
        out_shape=(
            jax.ShapeDtypeStruct((slots, channels), BF16),
            jax.ShapeDtypeStruct((8, length), F32),
        ),
        in_specs=[VMEM_SPEC] * 2,
        out_specs=(VMEM_SPEC, VMEM_SPEC),
        compiler_params=params(12),
        cost_estimate=cost(2 * slots * length * channels, 2 << 20),
        name="pack_cot",
    )(serial, cot)


def conv_kernel(nb_ref, below_ref, own_ref, above_ref, w_ref, slot_ref, g_ref, buf_ref, table, acc):
    step = pl.program_id(0)
    length, channels = own_ref.shape
    slots = buf_ref.shape[0]
    rows = table.shape[1]
    index = (lax.axis_index("z") * lax.axis_size("x") + lax.axis_index("x")) * lax.axis_size(
        "c"
    ) + lax.axis_index("c")
    base = index * length - RIM

    @pl.when(step == 0)
    def _():
        table[:, :RIM] = turned(below_ref[...]).astype(BF16)
        table[:, RIM : RIM + length] = turned(own_ref[...]).astype(BF16)
        table[:, RIM + length :] = turned(above_ref[...]).astype(BF16)
        acc[...] = jnp.zeros_like(acc)

    total = acc[...]
    for j in range(nb_ref.shape[0]):
        linked = nb_ref[j]
        local = jnp.where(linked < 0, -1, linked - base)
        pick = one_hot(iota((rows, length), 0) == local)
        gathered = mm(table[...], pick).astype(BF16)
        g_ref[j * channels : (j + 1) * channels, :] = gathered
        total = total + mm_tn(w_ref[j * channels : (j + 1) * channels, :], gathered)
    acc[...] = total

    @pl.when(step == pl.num_programs(0) - 1)
    def _():
        mixed = (own_ref[...].astype(F32) + turned(acc[...])).astype(BF16)
        pick = one_hot(iota((slots, length), 0) == slot_ref[0:1, :].astype(jnp.int32))
        buf_ref[...] = mm(pick, mixed).astype(BF16)


def gather_conv(nb, below, own, above, w_conv, slot, slots):
    length, channels = own.shape
    count = nb.shape[0]
    per = OFFSETS_PER_STEP
    rows = length + 2 * RIM
    whole = lambda *shape: pl.BlockSpec(shape, lambda i: (0,) * len(shape))
    return pl.pallas_call(
        conv_kernel,
        grid=(count // per,),
        out_shape=(
            jax.ShapeDtypeStruct((count * channels, length), BF16),
            jax.ShapeDtypeStruct((slots, channels), BF16),
        ),
        in_specs=[
            pl.BlockSpec((per, 1, length), lambda i: (i, 0, 0)),
            whole(RIM, channels),
            whole(length, channels),
            whole(RIM, channels),
            pl.BlockSpec((per * channels, channels), lambda i: (i, 0)),
            whole(8, length),
        ],
        out_specs=(
            pl.BlockSpec((per * channels, length), lambda i: (i, 0)),
            whole(slots, channels),
        ),
        scratch_shapes=[pltpu.VMEM((channels, rows), BF16), pltpu.VMEM((channels, length), F32)],
        compiler_params=params(32, dimension_semantics=("arbitrary",)),
        cost_estimate=cost(2 * count * length * channels * (rows + channels), 12 << 20),
        name="gather_conv",
    )(nb, below, own, above, w_conv, slot)


def arrive_kernel(cot_ref, w_ref, up_ref, datt_ref, datt_t_ref, row_ref, col_ref):
    slots, _ = cot_ref.shape
    length = up_ref.shape[0]
    arrived = cot_ref[...]
    valid = jnp.broadcast_to(arrived[:, 0:1].astype(F32), (slots, 128)) < VACANT / 2
    lower = one_hot(iota((slots, slots), 1) < iota((slots, slots), 0))
    ahead = mm(lower, one_hot(valid))
    col = jnp.where(valid, ahead, -1.0)
    col_ref[...] = col
    row = jnp.transpose(col, (1, 0))[0:8, :]
    row_ref[...] = row
    pick = one_hot(iota((length, slots), 0) == row[0:1, :].astype(jnp.int32))
    upstream = mm(pick, arrived).astype(BF16)
    up_ref[...] = upstream
    d_att = mm_nt(upstream, w_ref[...]).astype(BF16)
    datt_ref[...] = d_att
    datt_t_ref[...] = turned(d_att).astype(BF16)


def arrive(cot_buf, w_proj, length):
    slots, channels = cot_buf.shape
    return pl.pallas_call(
        arrive_kernel,
        out_shape=(
            jax.ShapeDtypeStruct((length, channels), BF16),
            jax.ShapeDtypeStruct((length, channels), BF16),
            jax.ShapeDtypeStruct((channels, length), BF16),
            jax.ShapeDtypeStruct((8, slots), F32),
            jax.ShapeDtypeStruct((slots, 128), F32),
        ),
        in_specs=[VMEM_SPEC] * 2,
        out_specs=(VMEM_SPEC,) * 5,
        compiler_params=params(16),
        cost_estimate=cost(2 * slots * length * channels * 3, 2 << 20),
        name="arrive",
    )(cot_buf, w_proj)


def patch_kernel(
    mix_ref,
    up_ref,
    datt_ref,
    datt_t_ref,
    row_ref,
    col_ref,
    wqkv_ref,
    wproj_ref,
    out_ref,
    dp_ref,
    gw_ref,
    att_t,
    dq_t,
    dk,
    dv,
):
    length, channels = up_ref.shape
    slots = mix_ref.shape[0]
    depth = channels // HEADS
    factor = depth ** (-0.5)
    group = 128
    pick = one_hot(iota((length, slots), 0) == row_ref[0:1, :].astype(jnp.int32))
    patched = mm(pick, mix_ref[...])
    values_t = turned(patched)
    centre_t = values_t - jnp.mean(values_t, axis=0, keepdims=True)
    inverse = lax.rsqrt(jnp.mean(centre_t * centre_t, axis=0, keepdims=True) + EPSILON)
    centred_t = centre_t * inverse
    normed_t = centred_t.astype(BF16)
    w_qkv = wqkv_ref[...]
    qkv_t = mm_tn(w_qkv, normed_t)
    q_t = (qkv_t[:channels] * factor).astype(BF16)
    k_t = qkv_t[channels : 2 * channels].astype(BF16)
    v_t = qkv_t[2 * channels :].astype(BF16)
    q = turned(q_t).astype(BF16)
    k = turned(k_t).astype(BF16)
    v = turned(v_t).astype(BF16)
    d_att = datt_ref[...]
    d_att_t = datt_t_ref[...]
    lane = iota((length, group), 1)
    sub = iota((group, length), 0)
    zero = jnp.zeros((), BF16)
    for g in range(channels // group):
        span = slice(g * group, (g + 1) * group)
        k_g, v_g = k[:, span], v[:, span]
        q_g, da_g = q[:, span], d_att[:, span]
        q_tg, da_tg = q_t[span], d_att_t[span]
        dk_g = jnp.zeros((length, group), F32)
        dv_g = jnp.zeros((length, group), F32)
        for h in range(group // depth):
            in_rows = lax.div(sub, jnp.int32(depth)) == h
            in_lanes = lax.div(lane, jnp.int32(depth)) == h
            at = g * group + h * depth
            scores = mm(k_g, jnp.where(in_rows, q_tg, zero))
            e = jnp.exp(scores - jnp.max(scores, axis=0, keepdims=True))
            p = e * (1.0 / jnp.sum(e, axis=0, keepdims=True))
            pb = p.astype(BF16)
            att_t[at : at + depth, :] = mm(v_t[at : at + depth], pb)
            dv_g = dv_g + mm(pb, jnp.where(in_lanes, da_g, zero))
            dp = mm(v_g, jnp.where(in_rows, da_tg, zero))
            ds = (p * (dp - jnp.sum(dp * p, axis=0, keepdims=True))).astype(BF16)
            dq_t[at : at + depth, :] = mm(k_t[at : at + depth], ds)
            dk_g = dk_g + mm(ds, jnp.where(in_lanes, q_g, zero))
        dk[:, span] = dk_g
        dv[:, span] = dv_g
    attended_t = att_t[...].astype(BF16)
    attended = turned(attended_t).astype(BF16)
    out_patch = (patched + mm(attended, wproj_ref[...])).astype(BF16)
    upstream = up_ref[...]
    gw_ref[:, 3 * channels :] = mm(attended_t, upstream)
    dq_t_full = dq_t[...] * factor
    dk_full, dv_full = dk[...], dv[...]
    gw_ref[:, :channels] = mm(normed_t, turned(dq_t_full).astype(BF16))
    gw_ref[:, channels : 2 * channels] = mm(normed_t, dk_full.astype(BF16))
    gw_ref[:, 2 * channels : 3 * channels] = mm(normed_t, dv_full.astype(BF16))
    d_norm = mm(w_qkv[:, :channels], dq_t_full.astype(BF16))
    d_norm = d_norm + mm(w_qkv[:, channels : 2 * channels], turned(dk_full).astype(BF16))
    d_norm = d_norm + mm(w_qkv[:, 2 * channels :], turned(dv_full).astype(BF16))
    d_layer = inverse * (
        d_norm
        - jnp.mean(d_norm, axis=0, keepdims=True)
        - centred_t * jnp.mean(d_norm * centred_t, axis=0, keepdims=True)
    )
    d_patch = (upstream.astype(F32) + turned(d_layer)).astype(BF16)
    key = jnp.broadcast_to(col_ref[:, 0:1].astype(jnp.int32), (slots, length))
    back = one_hot(iota((slots, length), 1) == key)
    dp_ref[...] = mm(back, d_patch).astype(BF16)
    out_ref[...] = mm(back, out_patch).astype(BF16)


def patch(mix_buf, up, d_att, d_att_t, row, col, w_qkv, w_proj):
    slots, channels = mix_buf.shape
    length = up.shape[0]
    return pl.pallas_call(
        patch_kernel,
        out_shape=(
            jax.ShapeDtypeStruct((slots, channels), BF16),
            jax.ShapeDtypeStruct((slots, channels), BF16),
            jax.ShapeDtypeStruct((channels, 4 * channels), F32),
        ),
        in_specs=[VMEM_SPEC] * 8,
        out_specs=(VMEM_SPEC,) * 3,
        scratch_shapes=[
            pltpu.VMEM((channels, length), F32),
            pltpu.VMEM((channels, length), F32),
            pltpu.VMEM((length, channels), F32),
            pltpu.VMEM((length, channels), F32),
        ],
        compiler_params=params(32),
        cost_estimate=cost(14e9, 4 << 20),
        name="patch",
    )(mix_buf, up, d_att, d_att_t, row, col, w_qkv, w_proj)


def unpack(slot, buf):
    slots = buf.shape[0]
    length = slot.shape[1]
    wide = jnp.transpose(jnp.broadcast_to(slot[0:1, :], (128, length)), (1, 0))
    key = jnp.broadcast_to(wide[:, 0:1].astype(jnp.int32), (length, slots))
    return mm(one_hot(iota((length, slots), 1) == key), buf).astype(BF16)


def output_kernel(slot_ref, buf_ref, out_ref):
    out_ref[...] = unpack(slot_ref[...], buf_ref[...])


def return_rows(slot, buf):
    length, channels = slot.shape[1], buf.shape[1]
    return pl.pallas_call(
        output_kernel,
        out_shape=jax.ShapeDtypeStruct((length, channels), BF16),
        in_specs=[VMEM_SPEC] * 2,
        out_specs=VMEM_SPEC,
        compiler_params=params(12),
        cost_estimate=cost(2 * length * buf.shape[0] * channels, 1 << 20),
        name="return_rows",
    )(slot, buf)


PIECE = 128
PART = 16


def grad_kernel(sizes, slot_ref, buf_ref, g_ref, gw_ref, keep_ref, send_ref, d_mixed, total):
    step = pl.program_id(0)
    nz, nx, nc, nrep = sizes
    block = g_ref.shape[0]
    channels = buf_ref.shape[1]

    @pl.when(step == 0)
    def _():
        d_mixed[...] = unpack(slot_ref[...], buf_ref[...])

    total[pl.ds(pl.multiple_of(step * block, block), block), :] = mm(g_ref[...], d_mixed[...])

    @pl.when(step == pl.num_programs(0) - 1)
    def _():
        mine = (lax.axis_index("z"), lax.axis_index("x"), lax.axis_index("c"), lax.axis_index("rep"))
        rows = total.shape[0] // (nz * nx * nc)
        fine = gw_ref.shape[0] // (nz * nx * nc)
        for core in range(nc):
            for is_mine, ref in ((True, keep_ref), (False, send_ref)):
                same = mine[2] == core

                @pl.when(same if is_mine else jnp.logical_not(same))
                def _(core=core, ref=ref):
                    for z in range(nz):
                        sz = lax.rem(z - mine[0] + nz, nz)
                        for x in range(nx):
                            sx = lax.rem(x - mine[1] + nx, nx)
                            d = (z * nx + x) * nc + core
                            for part in range(PIECE // PART):
                                half, y = part // nrep, part % nrep
                                sy = lax.rem(y - mine[3] + nrep, nrep)
                                first = part * PART
                                if part == PIECE // PART - 1:
                                    terms = [
                                        gw_ref[
                                            d * fine : (d + 1) * fine,
                                            j * channels : (j + 1) * channels,
                                        ]
                                        for j in range(4)
                                    ]
                                    value = jnp.concatenate(terms, axis=0)
                                elif first + PART <= rows:
                                    value = total[d * rows + first : d * rows + first + PART, :]
                                else:
                                    left = rows - first
                                    value = jnp.concatenate(
                                        [
                                            total[d * rows + first : d * rows + rows, :],
                                            jnp.zeros((PART - left, channels), F32),
                                        ],
                                        axis=0,
                                    )
                                lead = sx * nrep + sy if half == 0 else sy * nx + sx
                                ref[half, lead, sz] = value.astype(BF16)


def grad_terms(slot, buf, g, gw, sizes):
    slots, channels = buf.shape
    length = slot.shape[1]
    nz, nx, _, nrep = sizes
    block = 3 * channels
    whole = lambda *shape: pl.BlockSpec(shape, lambda i: (0,) * len(shape))
    shape = (2, nx * nrep, nz, PART, channels)
    return pl.pallas_call(
        functools.partial(grad_kernel, sizes),
        grid=(g.shape[0] // block,),
        out_shape=(jax.ShapeDtypeStruct(shape, BF16), jax.ShapeDtypeStruct(shape, BF16)),
        in_specs=[
            whole(8, length),
            whole(slots, channels),
            pl.BlockSpec((block, length), lambda i: (i, 0)),
            whole(*gw.shape),
        ],
        out_specs=(whole(*shape), whole(*shape)),
        scratch_shapes=[
            pltpu.VMEM((length, channels), BF16),
            pltpu.VMEM((g.shape[0], channels), F32),
        ],
        compiler_params=params(32, dimension_semantics=("arbitrary",)),
        cost_estimate=cost(2 * g.shape[0] * length * channels, 12 << 20),
        name="grad_terms",
    )(slot, buf, g, gw)


def add_kernel(plan, *refs):
    count = sum(len(sources) for sources, _ in plan)
    ins, outs = refs[:count], refs[count:]
    at, to = 0, 0
    for sources, parts in plan:
        group = ins[at : at + len(sources)]
        at += len(sources)
        for part in range(parts):
            value = None
            for ref, (lead, per) in zip(group, sources):
                term = ref[lead + part * per : lead + (part + 1) * per].astype(F32)
                value = term if value is None else value + term
            outs[to][...] = value.astype(BF16)
            to += 1


def pair_kernel(sides, count, *refs):
    ins, outs = refs[: 2 * count], refs[2 * count :]
    for part, out in enumerate(outs):
        for side in range(sides):
            value = None
            for ref in ins[side * count : (side + 1) * count]:
                term = ref[part].astype(F32)
                value = term if value is None else value + term
            rows = value.shape[0]
            out[side * rows : (side + 1) * rows, :] = value.astype(BF16)


def add_pairs(a, b):
    parts, rows, channels = a[0].shape
    shape = jax.ShapeDtypeStruct((2 * rows, channels), BF16)
    return pl.pallas_call(
        functools.partial(pair_kernel, 2, len(a)),
        out_shape=(shape,) * parts,
        in_specs=[VMEM_SPEC] * (2 * len(a)),
        out_specs=(VMEM_SPEC,) * parts,
        compiler_params=params(8),
        cost_estimate=cost(1 << 20, 1 << 20),
        name="add_pairs",
    )(*a, *b)


def add_up(terms):
    plan, arrays, shapes = [], [], []
    for sources, lead_rows, parts in terms:
        per = lead_rows // parts
        plan.append((tuple((lead, per) for _, lead in sources), parts))
        arrays += [a for a, _ in sources]
        tail = sources[0][0].shape[1:]
        shapes += [jax.ShapeDtypeStruct((per, *tail), BF16)] * parts
    nbytes = sum(2 * s.size for s in shapes) * 3
    return pl.pallas_call(
        functools.partial(add_kernel, tuple(plan)),
        out_shape=tuple(shapes),
        in_specs=[VMEM_SPEC] * len(arrays),
        out_specs=(VMEM_SPEC,) * len(shapes),
        compiler_params=params(16),
        cost_estimate=cost(nbytes, nbytes),
        name="add_up",
    )(*arrays)


def final_kernel(sizes, *refs):
    _, _, _, nrep = sizes
    ins, (conv_ref, qkv_ref, proj_ref, piece) = refs[:nrep], refs[nrep:]
    me = lax.axis_index("rep")
    rows, channels = conv_ref.shape
    fine = qkv_ref.shape[0]
    for s, ref in enumerate(ins):
        y = lax.rem(me - s + nrep, nrep)
        for half in range(2):
            start = pl.multiple_of((half * nrep + y) * PART, PART)
            piece[pl.ds(start, PART), :] = ref[half * PART : (half + 1) * PART, :].astype(F32)
    conv_ref[...] = piece[:rows, :]
    base = PIECE - PART
    for j in range(3):
        qkv_ref[:, j * channels : (j + 1) * channels] = piece[base + fine * j : base + fine * (j + 1), :]
    proj_ref[...] = piece[base + 3 * fine : base + 4 * fine, :]


def shifted(a, axis, by):
    size = lax.axis_size(axis)
    return lax.ppermute(a, axis, [(i, (i + by) % size) for i in range(size)])


def per_device(features, neighbours, serial, w_conv, w_qkv, w_proj, cotangent):
    feats = features[0]
    length, channels = feats.shape
    slab_count = lax.axis_size(SPACE)
    sizes = tuple(lax.axis_size(a) for a in ("z", "x", "c", "rep"))
    nz, nx, _, nrep = sizes
    capacity = 2 * length // slab_count
    slots = slab_count * capacity
    up = [(i, i + 1) for i in range(slab_count - 1)]
    down = [(j, i) for i, j in up]

    def exchange(buf):
        parts = buf.reshape(slab_count, capacity, channels)
        out = lax.all_to_all(parts, SPACE, split_axis=0, concat_axis=0, tiled=True)
        return out.reshape(slots, channels)

    below = lax.ppermute(feats[length - RIM :], SPACE, up)
    above = lax.ppermute(feats[:RIM], SPACE, down)
    cot_buf, slot = pack_cot(serial, cotangent[0], slots, capacity)
    cot_buf, below, above = lax.optimization_barrier((cot_buf, below, above))
    cot_in = exchange(cot_buf)
    nb = jnp.transpose(neighbours, (2, 0, 1))
    g, mix_buf = gather_conv(nb, below, feats, above, w_conv, slot, slots)
    mix_in = exchange(mix_buf)
    upstream, d_att, d_att_t, row, col = arrive(cot_in, w_proj, length)
    out_buf, dp_buf, gw = patch(mix_in, upstream, d_att, d_att_t, row, col, w_qkv, w_proj)
    dp_in = exchange(dp_buf)
    dp_in, out_buf = lax.optimization_barrier((dp_in, out_buf))
    out_in = exchange(out_buf)
    output = return_rows(slot, out_in)
    keep, send = grad_terms(slot, dp_in, g, gw, sizes)

    got = lax.ppermute(send, "c", [(0, 1), (1, 0)])
    flat = lambda a: a.reshape(2 * nx * nrep, nz, PART, channels)
    keep, got = flat(keep), flat(got)
    half = nx * nrep
    parts = add_up([([(keep, 0), (got, 0)], half, nx), ([(keep, half), (got, half)], half, nrep)])
    a, b = parts[:nx], parts[nx:]
    a_in = [shifted(a[s], "x", s) for s in range(1, nx)]
    b_in = [shifted(b[s], "rep", s) for s in range(1, nrep)]
    parts = add_up(
        [
            ([(t, 0) for t in [a[0], *a_in]], nrep, nrep),
            ([(t, 0) for t in [b[0], *b_in]], nx, nx),
        ]
    )
    a, b = parts[:nrep], parts[nrep:]
    a_in = [shifted(a[s], "rep", s) for s in range(1, nrep)]
    b_in = [shifted(b[s], "x", s) for s in range(1, nx)]

    def rows_of(t):
        return t.reshape(nz, PART, channels)

    ab = add_pairs([rows_of(t) for t in (a[0], *a_in)], [rows_of(t) for t in (b[0], *b_in)])
    ab_in = [shifted(ab[s], "z", s) for s in range(1, nz)]
    (own,) = add_up([([(t, 0) for t in [ab[0], *ab_in]], 2 * PART, 1)])
    everyone = [own] + [shifted(own, "rep", s) for s in range(1, nrep)]
    places = slab_count
    g_conv, g_qkv, g_proj = pl.pallas_call(
        functools.partial(final_kernel, sizes),
        out_shape=(
            jax.ShapeDtypeStruct((w_conv.shape[0] // places, channels), F32),
            jax.ShapeDtypeStruct((channels // places, 3 * channels), F32),
            jax.ShapeDtypeStruct((channels // places, channels), F32),
        ),
        in_specs=[VMEM_SPEC] * nrep,
        out_specs=(VMEM_SPEC,) * 3,
        scratch_shapes=[pltpu.VMEM((PIECE, channels), F32)],
        compiler_params=params(8),
        name="final",
    )(*everyone)
    return (output[None], g_conv, g_qkv, g_proj)


def solution(mesh):
    fine = Mesh(mesh.devices.reshape(8, 4, 2, 4), ("z", "x", "c", "rep"))

    return jax.shard_map(
        per_device,
        mesh=fine,
        in_specs=(
            P("rep", SPACE, None),
            P("rep", SPACE, None),
            P("rep", SPACE),
            P(),
            P(),
            P(),
            P("rep", SPACE, None),
        ),
        out_specs=(P("rep", SPACE, None), P(SPACE, None), P(SPACE, None), P(SPACE, None)),
        check_vma=False,
    )
```

```python
import functools

import jax
import jax.numpy as jnp
from jax import lax
from jax.experimental import pallas as pl
from jax.experimental.pallas import tpu as pltpu
from jax.sharding import Mesh
from jax.sharding import PartitionSpec as P


HEADS = 8
RIM = 128
EPSILON = 1e-05
SPACE = ("z", "x", "c")
VACANT = 512.0
OFFSETS_PER_STEP = 3

F32 = jnp.float32
BF16 = jnp.bfloat16


def iota(shape, dim):
    return lax.broadcasted_iota(jnp.int32, shape, dim)


def mm(a, b):
    return jnp.dot(a, b, preferred_element_type=F32)


def mm_nt(a, b):
    return lax.dot_general(a, b, (((1,), (1,)), ((), ())), preferred_element_type=F32)


def mm_tn(a, b):
    return lax.dot_general(a, b, (((0,), (0,)), ((), ())), preferred_element_type=F32)


def one_hot(mask):
    return jnp.where(mask, 1.0, 0.0).astype(BF16)


def turned(a):
    return jnp.transpose(a.astype(F32), (1, 0))


def cost(flops, nbytes):
    return pl.CostEstimate(flops=int(flops), bytes_accessed=int(nbytes), transcendentals=0)


VMEM_SPEC = pl.BlockSpec(memory_space=pltpu.VMEM)


def in_hbm(a):
    return pltpu.with_memory_space_constraint(a, pltpu.HBM)


def params(mebibytes, **more):
    return pltpu.CompilerParams(vmem_limit_bytes=mebibytes << 20, **more)


def slots_of(serial, capacity, owners):
    length = serial.shape[1]
    owner = lax.div(serial, jnp.int32(length))
    member = iota((owners, length), 0) == owner
    before = one_hot(iota((length, length), 0) < iota((length, length), 1))
    earlier = mm(one_hot(member), before)
    place = earlier + (capacity * iota((owners, length), 0)).astype(F32)
    return jnp.sum(jnp.where(member, place, 0.0), axis=0, keepdims=True)


def conv_kernel(
    capacity,
    serial_ref,
    cot_ref,
    nb_ref,
    below_ref,
    own_ref,
    above_ref,
    w_ref,
    g_ref,
    buf_ref,
    slot_ref,
    table,
    acc,
):
    step = pl.program_id(0)
    length, channels = own_ref.shape
    slots = buf_ref.shape[0]
    rows = table.shape[1]
    index = (lax.axis_index("z") * lax.axis_size("x") + lax.axis_index("x")) * lax.axis_size(
        "c"
    ) + lax.axis_index("c")
    base = index * length - RIM

    @pl.when(step == 0)
    def _():
        table[:, :RIM] = turned(below_ref[...]).astype(BF16)
        table[:, RIM : RIM + length] = turned(own_ref[...]).astype(BF16)
        table[:, RIM + length :] = turned(above_ref[...]).astype(BF16)
        acc[...] = jnp.zeros_like(acc)

    total = acc[...]
    for j in range(nb_ref.shape[0]):
        linked = nb_ref[j]
        local = jnp.where(linked < 0, -1, linked - base)
        pick = one_hot(iota((rows, length), 0) == local)
        gathered = mm(table[...], pick).astype(BF16)
        g_ref[j * channels : (j + 1) * channels, :] = gathered
        total = total + mm_tn(w_ref[j * channels : (j + 1) * channels, :], gathered)
    acc[...] = total

    @pl.when(step == pl.num_programs(0) - 1)
    def _():
        mixed = (own_ref[...].astype(F32) + turned(acc[...])).astype(BF16)
        slot = slots_of(serial_ref[...], capacity, slots // capacity)
        slot_ref[...] = jnp.broadcast_to(slot, slot_ref.shape)
        mask = iota((slots, length), 0) == slot.astype(jnp.int32)
        taken = jnp.sum(jnp.where(mask, 1.0, 0.0), axis=1, keepdims=True)
        vacant = jnp.where(taken > 0.5, 0.0, VACANT)
        pick = one_hot(mask)
        buf_ref[:, :channels] = mm(pick, mixed).astype(BF16)
        buf_ref[:, channels:] = (mm(pick, cot_ref[...]) + vacant).astype(BF16)


def gather_conv(serial, cot, nb, below, own, above, w_conv, slots, capacity):
    length, channels = own.shape
    count = nb.shape[0]
    per = OFFSETS_PER_STEP
    rows = length + 2 * RIM
    whole = lambda *shape: pl.BlockSpec(shape, lambda i: (0,) * len(shape))
    return pl.pallas_call(
        functools.partial(conv_kernel, capacity),
        grid=(count // per,),
        out_shape=(
            pltpu.HBM((count * channels, length), BF16),
            jax.ShapeDtypeStruct((slots, 2 * channels), BF16),
            jax.ShapeDtypeStruct((8, length), F32),
        ),
        in_specs=[
            whole(1, length),
            whole(length, channels),
            pl.BlockSpec((per, 1, length), lambda i: (i, 0, 0)),
            whole(RIM, channels),
            whole(length, channels),
            whole(RIM, channels),
            pl.BlockSpec((per * channels, channels), lambda i: (i, 0)),
        ],
        out_specs=(
            pl.BlockSpec((per * channels, length), lambda i: (i, 0)),
            whole(slots, 2 * channels),
            whole(8, length),
        ),
        scratch_shapes=[pltpu.VMEM((channels, rows), BF16), pltpu.VMEM((channels, length), F32)],
        compiler_params=params(32, dimension_semantics=("arbitrary",)),
        cost_estimate=cost(2 * count * length * channels * (rows + channels), 12 << 20),
        name="gather_conv",
    )(in_hbm(serial), in_hbm(cot), in_hbm(nb), below, in_hbm(own), above, in_hbm(w_conv))


def patch_kernel(
    buf_ref,
    wqkv_ref,
    wproj_ref,
    out_ref,
    dp_ref,
    gw_ref,
    key_s,
    value_s,
    query_s,
    datt_s,
    key_t,
    value_t,
    query_t,
    datt_t,
    att_t,
    dq_t,
    dk,
    dv,
):
    slots, channels = out_ref.shape
    groups, length, group = dk.shape
    depth = channels // HEADS
    factor = depth ** (-0.5)

    mark = buf_ref[:, channels : channels + 128][:, 0:1]
    valid = jnp.broadcast_to(mark.astype(F32), (slots, 128)) < VACANT / 2
    lower = one_hot(iota((slots, slots), 1) < iota((slots, slots), 0))
    col = jnp.where(valid, mm(lower, one_hot(valid)), -1.0)
    row = jnp.transpose(col, (1, 0))[0:1, :].astype(jnp.int32)
    rows = mm(one_hot(iota((length, slots), 0) == row), buf_ref[...])
    patched, upstream = rows[:, :channels], rows[:, channels:].astype(BF16)

    values_t = turned(patched)
    centre_t = values_t - jnp.mean(values_t, axis=0, keepdims=True)
    inverse = lax.rsqrt(jnp.mean(centre_t * centre_t, axis=0, keepdims=True) + EPSILON)
    centred_t = centre_t * inverse
    normed_t = centred_t.astype(BF16)
    w_qkv = wqkv_ref[...]
    qkv_t = mm_tn(w_qkv, normed_t)
    d_att = mm_nt(upstream, wproj_ref[...]).astype(BF16)
    query_t[...] = (qkv_t[:channels] * factor).astype(BF16)
    key_t[...] = qkv_t[channels : 2 * channels].astype(BF16)
    value_t[...] = qkv_t[2 * channels :].astype(BF16)
    datt_t[...] = turned(d_att).astype(BF16)
    for source, target in ((query_t, query_s), (key_t, key_s), (value_t, value_s)):
        flat = turned(source[...]).astype(BF16)
        for g in range(groups):
            target[g] = flat[:, g * group : (g + 1) * group]
    for g in range(groups):
        datt_s[g] = d_att[:, g * group : (g + 1) * group]

    lane = iota((length, group), 1)
    sub = iota((group, length), 0)
    zero = jnp.zeros((), BF16)

    def heads_of(g, carry):
        start = pl.multiple_of(g * group, group)
        k_g, v_g, q_g, da_g = key_s[g], value_s[g], query_s[g], datt_s[g]
        q_tg, da_tg = query_t[pl.ds(start, group), :], datt_t[pl.ds(start, group), :]
        dk_g = jnp.zeros((length, group), F32)
        dv_g = jnp.zeros((length, group), F32)
        for h in range(group // depth):
            in_rows = lax.div(sub, jnp.int32(depth)) == h
            in_lanes = lax.div(lane, jnp.int32(depth)) == h
            at = pl.ds(pl.multiple_of(start + h * depth, depth), depth)
            scores = mm(k_g, jnp.where(in_rows, q_tg, zero))
            e = jnp.exp(scores - jnp.max(scores, axis=0, keepdims=True))
            p = e * (1.0 / jnp.sum(e, axis=0, keepdims=True))
            pb = p.astype(BF16)
            att_t[at, :] = mm(value_t[at, :], pb)
            dv_g = dv_g + mm(pb, jnp.where(in_lanes, da_g, zero))
            dp = mm(v_g, jnp.where(in_rows, da_tg, zero))
            ds = (p * (dp - jnp.sum(dp * p, axis=0, keepdims=True))).astype(BF16)
            dq_t[at, :] = mm(key_t[at, :], ds)
            dk_g = dk_g + mm(ds, jnp.where(in_lanes, q_g, zero))
        dk[g] = dk_g
        dv[g] = dv_g
        return carry

    lax.fori_loop(0, groups, heads_of, 0)

    attended_t = att_t[...].astype(BF16)
    out_patch = (patched + mm(turned(attended_t).astype(BF16), wproj_ref[...])).astype(BF16)
    gw_ref[:, 3 * channels :] = mm(attended_t, upstream)
    dq_full = dq_t[...] * factor
    gw_ref[:, :channels] = mm(normed_t, turned(dq_full).astype(BF16))
    d_norm = mm(w_qkv[:, :channels], dq_full.astype(BF16))
    for part, ref in ((1, dk), (2, dv)):
        for g in range(groups):
            at = part * channels + g * group
            grads = ref[g]
            gw_ref[:, at : at + group] = mm(normed_t, grads.astype(BF16))
            d_norm = d_norm + mm(w_qkv[:, at : at + group], turned(grads).astype(BF16))
    d_layer = inverse * (
        d_norm
        - jnp.mean(d_norm, axis=0, keepdims=True)
        - centred_t * jnp.mean(d_norm * centred_t, axis=0, keepdims=True)
    )
    d_patch = (upstream.astype(F32) + turned(d_layer)).astype(BF16)
    key = jnp.broadcast_to(col[:, 0:1].astype(jnp.int32), (slots, length))
    back = one_hot(iota((slots, length), 1) == key)
    dp_ref[...] = mm(back, d_patch).astype(BF16)
    out_ref[...] = mm(back, out_patch).astype(BF16)


def patch(buf, w_qkv, w_proj, length):
    slots, channels = buf.shape[0], buf.shape[1] // 2
    group = 128
    groups = channels // group
    return pl.pallas_call(
        patch_kernel,
        out_shape=(
            jax.ShapeDtypeStruct((slots, channels), BF16),
            jax.ShapeDtypeStruct((slots, channels), BF16),
            jax.ShapeDtypeStruct((channels, 4 * channels), F32),
        ),
        in_specs=[VMEM_SPEC] * 3,
        out_specs=(VMEM_SPEC,) * 3,
        scratch_shapes=[pltpu.VMEM((groups, length, group), BF16)] * 4
        + [pltpu.VMEM((channels, length), BF16)] * 4
        + [pltpu.VMEM((channels, length), F32)] * 2
        + [pltpu.VMEM((groups, length, group), F32)] * 2,
        compiler_params=params(32),
        cost_estimate=cost(14e9, 4 << 20),
        name="patch",
    )(buf, w_qkv, w_proj)


def unpack(slot, buf):
    slots = buf.shape[0]
    length = slot.shape[1]
    wide = jnp.transpose(jnp.broadcast_to(slot[0:1, :], (128, length)), (1, 0))
    key = jnp.broadcast_to(wide[:, 0:1].astype(jnp.int32), (length, slots))
    return mm(one_hot(iota((length, slots), 1) == key), buf).astype(BF16)


def output_kernel(slot_ref, buf_ref, out_ref):
    out_ref[...] = unpack(slot_ref[...], buf_ref[...])


def return_rows(slot, buf):
    length, channels = slot.shape[1], buf.shape[1]
    return pl.pallas_call(
        output_kernel,
        out_shape=jax.ShapeDtypeStruct((length, channels), BF16),
        in_specs=[VMEM_SPEC] * 2,
        out_specs=VMEM_SPEC,
        compiler_params=params(12),
        cost_estimate=cost(2 * length * buf.shape[0] * channels, 1 << 20),
        name="return_rows",
    )(slot, buf)


PIECE = 128
PART = 16


def grad_kernel(sizes, slot_ref, buf_ref, g_ref, gw_ref, keep_ref, send_ref, d_mixed, total):
    step = pl.program_id(0)
    nz, nx, nc, nrep = sizes
    block = g_ref.shape[0]
    channels = buf_ref.shape[1]

    @pl.when(step == 0)
    def _():
        d_mixed[...] = unpack(slot_ref[...], buf_ref[...])

    total[pl.ds(pl.multiple_of(step * block, block), block), :] = mm(g_ref[...], d_mixed[...])

    @pl.when(step == pl.num_programs(0) - 1)
    def _():
        mine = (lax.axis_index("z"), lax.axis_index("x"), lax.axis_index("c"), lax.axis_index("rep"))
        rows = total.shape[0] // (nz * nx * nc)
        fine = gw_ref.shape[0] // (nz * nx * nc)
        for core in range(nc):
            for is_mine, ref in ((True, keep_ref), (False, send_ref)):
                same = mine[2] == core

                @pl.when(same if is_mine else jnp.logical_not(same))
                def _(core=core, ref=ref):
                    for z in range(nz):
                        sz = lax.rem(z - mine[0] + nz, nz)
                        for x in range(nx):
                            sx = lax.rem(x - mine[1] + nx, nx)
                            d = (z * nx + x) * nc + core
                            for part in range(PIECE // PART):
                                half, y = part // nrep, part % nrep
                                sy = lax.rem(y - mine[3] + nrep, nrep)
                                first = part * PART
                                if part == PIECE // PART - 1:
                                    terms = [
                                        gw_ref[
                                            d * fine : (d + 1) * fine,
                                            j * channels : (j + 1) * channels,
                                        ]
                                        for j in range(4)
                                    ]
                                    value = jnp.concatenate(terms, axis=0)
                                elif first + PART <= rows:
                                    value = total[d * rows + first : d * rows + first + PART, :]
                                else:
                                    left = rows - first
                                    value = jnp.concatenate(
                                        [
                                            total[d * rows + first : d * rows + rows, :],
                                            jnp.zeros((PART - left, channels), F32),
                                        ],
                                        axis=0,
                                    )
                                lead = sx * nrep + sy if half == 0 else sy * nx + sx
                                ref[half, lead, sz] = value.astype(BF16)


def grad_terms(slot, buf, g, gw, sizes):
    slots, channels = buf.shape
    length = slot.shape[1]
    nz, nx, _, nrep = sizes
    block = 3 * channels
    whole = lambda *shape: pl.BlockSpec(shape, lambda i: (0,) * len(shape))
    shape = (2, nx * nrep, nz, PART, channels)
    return pl.pallas_call(
        functools.partial(grad_kernel, sizes),
        grid=(g.shape[0] // block,),
        out_shape=(jax.ShapeDtypeStruct(shape, BF16), jax.ShapeDtypeStruct(shape, BF16)),
        in_specs=[
            whole(8, length),
            whole(slots, channels),
            pl.BlockSpec((block, length), lambda i: (i, 0)),
            whole(*gw.shape),
        ],
        out_specs=(whole(*shape), whole(*shape)),
        scratch_shapes=[
            pltpu.VMEM((length, channels), BF16),
            pltpu.VMEM((g.shape[0], channels), F32),
        ],
        compiler_params=params(32, dimension_semantics=("arbitrary",)),
        cost_estimate=cost(2 * g.shape[0] * length * channels, 12 << 20),
        name="grad_terms",
    )(slot, buf, in_hbm(g), gw)


def add_kernel(plan, *refs):
    count = sum(len(sources) for sources, _ in plan)
    ins, outs = refs[:count], refs[count:]
    at, to = 0, 0
    for sources, parts in plan:
        group = ins[at : at + len(sources)]
        at += len(sources)
        for part in range(parts):
            value = None
            for ref, (lead, per) in zip(group, sources):
                term = ref[lead + part * per : lead + (part + 1) * per].astype(F32)
                value = term if value is None else value + term
            outs[to][...] = value.astype(BF16)
            to += 1


def pair_kernel(sides, count, *refs):
    ins, outs = refs[: 2 * count], refs[2 * count :]
    for part, out in enumerate(outs):
        for side in range(sides):
            value = None
            for ref in ins[side * count : (side + 1) * count]:
                term = ref[part].astype(F32)
                value = term if value is None else value + term
            rows = value.shape[0]
            out[side * rows : (side + 1) * rows, :] = value.astype(BF16)


def add_pairs(a, b):
    parts, rows, channels = a[0].shape
    shape = jax.ShapeDtypeStruct((2 * rows, channels), BF16)
    return pl.pallas_call(
        functools.partial(pair_kernel, 2, len(a)),
        out_shape=(shape,) * parts,
        in_specs=[VMEM_SPEC] * (2 * len(a)),
        out_specs=(VMEM_SPEC,) * parts,
        compiler_params=params(8),
        cost_estimate=cost(1 << 20, 1 << 20),
        name="add_pairs",
    )(*a, *b)


def add_up(terms):
    plan, arrays, shapes = [], [], []
    for sources, lead_rows, parts in terms:
        per = lead_rows // parts
        plan.append((tuple((lead, per) for _, lead in sources), parts))
        arrays += [a for a, _ in sources]
        tail = sources[0][0].shape[1:]
        shapes += [jax.ShapeDtypeStruct((per, *tail), BF16)] * parts
    nbytes = sum(2 * s.size for s in shapes) * 3
    return pl.pallas_call(
        functools.partial(add_kernel, tuple(plan)),
        out_shape=tuple(shapes),
        in_specs=[VMEM_SPEC] * len(arrays),
        out_specs=(VMEM_SPEC,) * len(shapes),
        compiler_params=params(16),
        cost_estimate=cost(nbytes, nbytes),
        name="add_up",
    )(*arrays)


def final_kernel(sizes, *refs):
    _, _, _, nrep = sizes
    ins, (conv_ref, qkv_ref, proj_ref, piece) = refs[:nrep], refs[nrep:]
    me = lax.axis_index("rep")
    rows, channels = conv_ref.shape
    fine = qkv_ref.shape[0]
    for s, ref in enumerate(ins):
        y = lax.rem(me - s + nrep, nrep)
        for half in range(2):
            start = pl.multiple_of((half * nrep + y) * PART, PART)
            piece[pl.ds(start, PART), :] = ref[half * PART : (half + 1) * PART, :].astype(F32)
    conv_ref[...] = piece[:rows, :]
    base = PIECE - PART
    for j in range(3):
        qkv_ref[:, j * channels : (j + 1) * channels] = piece[base + fine * j : base + fine * (j + 1), :]
    proj_ref[...] = piece[base + 3 * fine : base + 4 * fine, :]


def shifted(a, axis, by):
    size = lax.axis_size(axis)
    return lax.ppermute(a, axis, [(i, (i + by) % size) for i in range(size)])


def per_device(features, neighbours, serial, w_conv, w_qkv, w_proj, cotangent):
    feats = features[0]
    length, channels = feats.shape
    slab_count = lax.axis_size(SPACE)
    sizes = tuple(lax.axis_size(a) for a in ("z", "x", "c", "rep"))
    nz, nx, _, nrep = sizes
    capacity = 2 * length // slab_count
    slots = slab_count * capacity
    up = [(i, i + 1) for i in range(slab_count - 1)]
    down = [(j, i) for i, j in up]

    def exchange(buf):
        parts = buf.reshape(slab_count, capacity, -1)
        out = lax.all_to_all(parts, SPACE, split_axis=0, concat_axis=0, tiled=True)
        return out.reshape(slots, -1)

    below = lax.ppermute(feats[length - RIM :], SPACE, up)
    above = lax.ppermute(feats[:RIM], SPACE, down)
    nb = jnp.transpose(neighbours, (2, 0, 1))
    g, row_buf, slot = gather_conv(
        serial, cotangent[0], nb, below, feats, above, w_conv, slots, capacity
    )
    out_buf, dp_buf, gw = patch(exchange(row_buf), w_qkv, w_proj, length)
    keep, send = grad_terms(slot, exchange(dp_buf), g, gw, sizes)

    got = lax.ppermute(send, "c", [(0, 1), (1, 0)])
    flat = lambda a: a.reshape(2 * nx * nrep, nz, PART, channels)
    keep, got = flat(keep), flat(got)
    half = nx * nrep
    parts = add_up([([(keep, 0), (got, 0)], half, nx), ([(keep, half), (got, half)], half, nrep)])
    *parts, out_buf = lax.optimization_barrier((*parts, out_buf))
    a, b = parts[:nx], parts[nx:]
    a_in = [shifted(a[s], "x", s) for s in range(1, nx)]
    b_in = [shifted(b[s], "rep", s) for s in range(1, nrep)]
    out_in = exchange(out_buf)
    output = return_rows(slot, out_in)
    parts = add_up(
        [
            ([(t, 0) for t in [a[0], *a_in]], nrep, nrep),
            ([(t, 0) for t in [b[0], *b_in]], nx, nx),
        ]
    )
    a, b = parts[:nrep], parts[nrep:]
    a_in = [shifted(a[s], "rep", s) for s in range(1, nrep)]
    b_in = [shifted(b[s], "x", s) for s in range(1, nx)]

    def rows_of(t):
        return t.reshape(nz, PART, channels)

    ab = add_pairs([rows_of(t) for t in (a[0], *a_in)], [rows_of(t) for t in (b[0], *b_in)])
    ab_in = [shifted(ab[s], "z", s) for s in range(1, nz)]
    (own,) = add_up([([(t, 0) for t in [ab[0], *ab_in]], 2 * PART, 1)])
    everyone = [own] + [shifted(own, "rep", s) for s in range(1, nrep)]
    places = slab_count
    g_conv, g_qkv, g_proj = pl.pallas_call(
        functools.partial(final_kernel, sizes),
        out_shape=(
            jax.ShapeDtypeStruct((w_conv.shape[0] // places, channels), F32),
            jax.ShapeDtypeStruct((channels // places, 3 * channels), F32),
            jax.ShapeDtypeStruct((channels // places, channels), F32),
        ),
        in_specs=[VMEM_SPEC] * nrep,
        out_specs=(VMEM_SPEC,) * 3,
        scratch_shapes=[pltpu.VMEM((PIECE, channels), F32)],
        compiler_params=params(8),
        name="final",
    )(*everyone)
    return (output[None], g_conv, g_qkv, g_proj)


def solution(mesh):
    fine = Mesh(mesh.devices.reshape(8, 4, 2, 4), ("z", "x", "c", "rep"))

    return jax.shard_map(
        per_device,
        mesh=fine,
        in_specs=(
            P("rep", SPACE, None),
            P("rep", SPACE, None),
            P("rep", SPACE),
            P(),
            P(),
            P(),
            P("rep", SPACE, None),
        ),
        out_specs=(P("rep", SPACE, None), P(SPACE, None), P(SPACE, None), P(SPACE, None)),
        check_vma=False,
    )
```

```python
import functools

import jax
import jax.numpy as jnp
from jax import lax
from jax.experimental import pallas as pl
from jax.experimental.pallas import tpu as pltpu
from jax.sharding import Mesh
from jax.sharding import PartitionSpec as P


HEADS = 8
RIM = 128
EPSILON = 1e-05
SPACE = ("z", "x", "c")
VACANT = 512.0
OFFSETS_PER_STEP = 3

F32 = jnp.float32
BF16 = jnp.bfloat16


def iota(shape, dim):
    return lax.broadcasted_iota(jnp.int32, shape, dim)


def mm(a, b):
    return jnp.dot(a, b, preferred_element_type=F32)


def mm_nt(a, b):
    return lax.dot_general(a, b, (((1,), (1,)), ((), ())), preferred_element_type=F32)


def mm_tn(a, b):
    return lax.dot_general(a, b, (((0,), (0,)), ((), ())), preferred_element_type=F32)


def one_hot(mask):
    return jnp.where(mask, 1.0, 0.0).astype(BF16)


def turned(a):
    return jnp.transpose(a.astype(F32), (1, 0))


def cost(flops, nbytes):
    return pl.CostEstimate(flops=int(flops), bytes_accessed=int(nbytes), transcendentals=0)


VMEM_SPEC = pl.BlockSpec(memory_space=pltpu.VMEM)


def in_hbm(a):
    return pltpu.with_memory_space_constraint(a, pltpu.HBM)


def params(mebibytes, **more):
    return pltpu.CompilerParams(vmem_limit_bytes=mebibytes << 20, **more)


def slots_of(serial, capacity, owners):
    length = serial.shape[1]
    owner = lax.div(serial, jnp.int32(length))
    member = iota((owners, length), 0) == owner
    before = one_hot(iota((length, length), 0) < iota((length, length), 1))
    earlier = mm(one_hot(member), before)
    place = earlier + (capacity * iota((owners, length), 0)).astype(F32)
    return jnp.sum(jnp.where(member, place, 0.0), axis=0, keepdims=True)


def pack_kernel(capacity, serial_ref, cot_ref, own_ref, buf_ref, slot_ref, own_t_ref):
    length, _ = cot_ref.shape
    slots = buf_ref.shape[0]
    slot = slots_of(serial_ref[...], capacity, slots // capacity)
    slot_ref[...] = jnp.broadcast_to(slot, slot_ref.shape)
    mask = iota((slots, length), 0) == slot.astype(jnp.int32)
    taken = jnp.sum(jnp.where(mask, 1.0, 0.0), axis=1, keepdims=True)
    vacant = jnp.where(taken > 0.5, 0.0, VACANT)
    buf_ref[...] = (mm(one_hot(mask), cot_ref[...]) + vacant).astype(BF16)
    own_t_ref[...] = turned(own_ref[...]).astype(BF16)


def whole(*shape):
    return pl.BlockSpec(shape, lambda i: (0,) * len(shape))


def pack_cot(serial, cot, own, slots, capacity):
    length, channels = cot.shape
    return pl.pallas_call(
        functools.partial(pack_kernel, capacity),
        grid=(1,),
        out_shape=(
            jax.ShapeDtypeStruct((slots, channels), BF16),
            jax.ShapeDtypeStruct((8, length), F32),
            jax.ShapeDtypeStruct((channels, length), BF16),
        ),
        in_specs=[whole(1, length), whole(length, channels), whole(length, channels)],
        out_specs=(whole(slots, channels), whole(8, length), whole(channels, length)),
        compiler_params=params(12),
        cost_estimate=cost(2 * slots * length * channels, 2 << 20),
        name="pack_cot",
    )(in_hbm(serial), in_hbm(cot), in_hbm(own))


def conv_kernel(
    nb_ref,
    slot_ref,
    cot_ref,
    below_ref,
    own_t_ref,
    above_ref,
    own_ref,
    w_ref,
    g_ref,
    buf_ref,
    table,
    held,
    acc,
):
    step = pl.program_id(0)
    last = pl.num_programs(0) - 1
    length, channels = own_ref.shape
    slots = buf_ref.shape[0]
    rows = table.shape[1]
    index = (lax.axis_index("z") * lax.axis_size("x") + lax.axis_index("x")) * lax.axis_size(
        "c"
    ) + lax.axis_index("c")
    base = index * length - RIM

    def gather():
        for j in range(nb_ref.shape[0]):
            linked = nb_ref[j]
            local = jnp.where(linked < 0, -1, linked - base)
            pick = one_hot(iota((rows, length), 0) == local)
            gathered = mm(table[...], pick).astype(BF16)
            g_ref[j * channels : (j + 1) * channels, :] = gathered
            held[j * channels : (j + 1) * channels, :] = gathered

    @pl.when(step == 0)
    def _():
        table[:, :RIM] = turned(below_ref[...]).astype(BF16)
        table[:, RIM : RIM + length] = own_t_ref[...]
        table[:, RIM + length :] = turned(above_ref[...]).astype(BF16)
        acc[...] = jnp.zeros_like(acc)
        gather()

    @pl.when(jnp.logical_and(step > 0, step < last))
    def _():
        acc[...] += mm_tn(w_ref[...], held[...])
        gather()

    @pl.when(step == last)
    def _():
        total = acc[...] + mm_tn(w_ref[...], held[...])
        mixed = (own_ref[...].astype(F32) + turned(total)).astype(BF16)
        pick = one_hot(iota((slots, length), 0) == slot_ref[0:1, :].astype(jnp.int32))
        buf_ref[:, :channels] = mm(pick, mixed).astype(BF16)
        buf_ref[:, channels:] = cot_ref[...]


def gather_conv(nb, slot, cot_buf, below, own_t, above, own, w_conv):
    length, channels = own.shape
    slots = cot_buf.shape[0]
    count = nb.shape[0]
    per = OFFSETS_PER_STEP
    steps = count // per
    rows = length + 2 * RIM
    return pl.pallas_call(
        conv_kernel,
        grid=(steps + 1,),
        out_shape=(
            pltpu.HBM((count * channels, length), BF16),
            jax.ShapeDtypeStruct((slots, 2 * channels), BF16),
        ),
        in_specs=[
            pl.BlockSpec((per, 1, length), lambda i: (jnp.minimum(i, steps - 1), 0, 0)),
            whole(8, length),
            whole(slots, channels),
            whole(RIM, channels),
            whole(channels, length),
            whole(RIM, channels),
            whole(length, channels),
            pl.BlockSpec((per * channels, channels), lambda i: (jnp.maximum(i - 1, 0), 0)),
        ],
        out_specs=(
            pl.BlockSpec((per * channels, length), lambda i: (jnp.minimum(i, steps - 1), 0)),
            whole(slots, 2 * channels),
        ),
        scratch_shapes=[
            pltpu.VMEM((channels, rows), BF16),
            pltpu.VMEM((per * channels, length), BF16),
            pltpu.VMEM((channels, length), F32),
        ],
        compiler_params=params(32, dimension_semantics=("arbitrary",)),
        cost_estimate=cost(2 * count * length * channels * (rows + channels), 12 << 20),
        name="gather_conv",
    )(in_hbm(nb), slot, cot_buf, below, own_t, above, in_hbm(own), in_hbm(w_conv))


def patch_kernel(
    buf_ref,
    wqkv_ref,
    wproj_ref,
    out_ref,
    dp_ref,
    gw_ref,
    key_s,
    value_s,
    query_s,
    datt_s,
    key_t,
    value_t,
    query_t,
    datt_t,
    att_t,
    dq_t,
    dk,
    dv,
):
    slots, channels = dp_ref.shape
    groups, length, group = dk.shape
    depth = channels // HEADS
    factor = depth ** (-0.5)

    mark = buf_ref[:, channels : channels + 128][:, 0:1]
    valid = jnp.broadcast_to(mark.astype(F32), (slots, 128)) < VACANT / 2
    lower = one_hot(iota((slots, slots), 1) < iota((slots, slots), 0))
    col = jnp.where(valid, mm(lower, one_hot(valid)), -1.0)
    row = jnp.transpose(col, (1, 0))[0:1, :].astype(jnp.int32)
    rows = mm(one_hot(iota((length, slots), 0) == row), buf_ref[...])
    patched, upstream = rows[:, :channels], rows[:, channels:].astype(BF16)

    values_t = turned(patched)
    centre_t = values_t - jnp.mean(values_t, axis=0, keepdims=True)
    inverse = lax.rsqrt(jnp.mean(centre_t * centre_t, axis=0, keepdims=True) + EPSILON)
    centred_t = centre_t * inverse
    normed_t = centred_t.astype(BF16)
    w_qkv = wqkv_ref[...]
    qkv_t = mm_tn(w_qkv, normed_t)
    d_att = mm_nt(upstream, wproj_ref[...]).astype(BF16)
    query_t[...] = (qkv_t[:channels] * factor).astype(BF16)
    key_t[...] = qkv_t[channels : 2 * channels].astype(BF16)
    value_t[...] = qkv_t[2 * channels :].astype(BF16)
    datt_t[...] = turned(d_att).astype(BF16)
    for source, target in ((query_t, query_s), (key_t, key_s), (value_t, value_s)):
        flat = turned(source[...]).astype(BF16)
        for g in range(groups):
            target[g] = flat[:, g * group : (g + 1) * group]
    for g in range(groups):
        datt_s[g] = d_att[:, g * group : (g + 1) * group]

    lane = iota((length, group), 1)
    sub = iota((group, length), 0)
    zero = jnp.zeros((), BF16)

    def heads_of(g, carry):
        start = pl.multiple_of(g * group, group)
        k_g, v_g, q_g, da_g = key_s[g], value_s[g], query_s[g], datt_s[g]
        q_tg, da_tg = query_t[pl.ds(start, group), :], datt_t[pl.ds(start, group), :]
        dk_g = jnp.zeros((length, group), F32)
        dv_g = jnp.zeros((length, group), F32)
        for h in range(group // depth):
            in_rows = lax.div(sub, jnp.int32(depth)) == h
            in_lanes = lax.div(lane, jnp.int32(depth)) == h
            at = pl.ds(pl.multiple_of(start + h * depth, depth), depth)
            scores = mm(k_g, jnp.where(in_rows, q_tg, zero))
            e = jnp.exp(scores - jnp.max(scores, axis=0, keepdims=True))
            p = e * (1.0 / jnp.sum(e, axis=0, keepdims=True))
            pb = p.astype(BF16)
            attended = mm(value_t[at, :], pb)
            att_t[at, :] = attended
            dv_g = dv_g + mm(pb, jnp.where(in_lanes, da_g, zero))
            dp = mm(v_g, jnp.where(in_rows, da_tg, zero))
            row_term = jnp.sum(datt_t[at, :].astype(F32) * attended, axis=0, keepdims=True)
            ds = (p * (dp - row_term)).astype(BF16)
            dq_t[at, :] = mm(key_t[at, :], ds)
            dk_g = dk_g + mm(ds, jnp.where(in_lanes, q_g, zero))
        dk[g] = dk_g
        dv[g] = dv_g
        return carry

    lax.fori_loop(0, groups, heads_of, 0)

    attended_t = att_t[...].astype(BF16)
    out_patch = (patched + mm(turned(attended_t).astype(BF16), wproj_ref[...])).astype(BF16)
    gw_ref[:, 3 * channels :] = mm(attended_t, upstream)
    dq_full = dq_t[...] * factor
    gw_ref[:, :channels] = mm(normed_t, turned(dq_full).astype(BF16))
    d_norm = mm(w_qkv[:, :channels], dq_full.astype(BF16))
    for part, ref in ((1, dk), (2, dv)):
        for g in range(groups):
            at = part * channels + g * group
            grads = ref[g]
            gw_ref[:, at : at + group] = mm(normed_t, grads.astype(BF16))
            d_norm = d_norm + mm(w_qkv[:, at : at + group], turned(grads).astype(BF16))
    d_layer = inverse * (
        d_norm
        - jnp.mean(d_norm, axis=0, keepdims=True)
        - centred_t * jnp.mean(d_norm * centred_t, axis=0, keepdims=True)
    )
    d_patch = (upstream.astype(F32) + turned(d_layer)).astype(BF16)
    key = jnp.broadcast_to(col[:, 0:1].astype(jnp.int32), (slots, length))
    back = one_hot(iota((slots, length), 1) == key)
    dp_ref[...] = mm(back, d_patch).astype(BF16)
    out_ref[...] = mm(back, out_patch).astype(BF16)


def patch(buf, w_qkv, w_proj, length):
    slots, channels = buf.shape[0], buf.shape[1] // 2
    group = 128
    groups = channels // group
    return pl.pallas_call(
        patch_kernel,
        out_shape=(
            jax.ShapeDtypeStruct((slots, channels), BF16),
            jax.ShapeDtypeStruct((slots, channels), BF16),
            jax.ShapeDtypeStruct((channels, 4 * channels), F32),
        ),
        in_specs=[VMEM_SPEC] * 3,
        out_specs=(VMEM_SPEC,) * 3,
        scratch_shapes=[pltpu.VMEM((groups, length, group), BF16)] * 4
        + [pltpu.VMEM((channels, length), BF16)] * 4
        + [pltpu.VMEM((channels, length), F32)] * 2
        + [pltpu.VMEM((groups, length, group), F32)] * 2,
        compiler_params=params(32),
        cost_estimate=cost(14e9, 4 << 20),
        name="patch",
    )(buf, w_qkv, w_proj)


def unpack(slot, buf):
    slots = buf.shape[0]
    length = slot.shape[1]
    wide = jnp.transpose(jnp.broadcast_to(slot[0:1, :], (128, length)), (1, 0))
    key = jnp.broadcast_to(wide[:, 0:1].astype(jnp.int32), (length, slots))
    return mm(one_hot(iota((length, slots), 1) == key), buf).astype(BF16)


def output_kernel(slot_ref, buf_ref, out_ref):
    out_ref[...] = unpack(slot_ref[...], buf_ref[...])


def return_rows(slot, buf):
    length, channels = slot.shape[1], buf.shape[1]
    return pl.pallas_call(
        output_kernel,
        out_shape=jax.ShapeDtypeStruct((length, channels), BF16),
        in_specs=[VMEM_SPEC] * 2,
        out_specs=VMEM_SPEC,
        compiler_params=params(12),
        cost_estimate=cost(2 * length * buf.shape[0] * channels, 1 << 20),
        name="return_rows",
    )(slot, buf)


GRAD_STEPS = 9
PIECE = 128
PART = 16


def grad_kernel(
    sizes, slot_ref, buf_ref, g_ref, gw_ref, keep_ref, send_ref, d_mixed, total, near, sems
):
    step = pl.program_id(0)
    nz, nx, nc, nrep = sizes
    block = g_ref.shape[0] // GRAD_STEPS
    channels = buf_ref.shape[1]

    def fetch(i):
        at = pl.ds(pl.multiple_of(i * block, block), block)
        return pltpu.make_async_copy(g_ref.at[at, :], near.at[at, :], sems.at[i])

    @pl.when(step == 0)
    def _():
        for i in range(GRAD_STEPS):
            fetch(i).start()
        d_mixed[...] = unpack(slot_ref[...], buf_ref[...])

    fetch(step).wait()
    at = pl.ds(pl.multiple_of(step * block, block), block)
    total[at, :] = mm(near[at, :], d_mixed[...])

    @pl.when(step == pl.num_programs(0) - 1)
    def _():
        mine = (lax.axis_index("z"), lax.axis_index("x"), lax.axis_index("c"), lax.axis_index("rep"))
        rows = total.shape[0] // (nz * nx * nc)
        fine = gw_ref.shape[0] // (nz * nx * nc)
        for core in range(nc):
            for is_mine, ref in ((True, keep_ref), (False, send_ref)):
                same = mine[2] == core

                @pl.when(same if is_mine else jnp.logical_not(same))
                def _(core=core, ref=ref):
                    for z in range(nz):
                        pair = lax.rem(z % 2 + lax.rem(mine[0], 2), 2)
                        four = lax.rem(z // 2 - lax.div(mine[0], 2) + nz // 2, nz // 2)
                        sz = pair * (nz // 2) + four
                        for x in range(nx):
                            sx = lax.rem(x - mine[1] + nx, nx)
                            d = (z * nx + x) * nc + core
                            for part in range(PIECE // PART):
                                half, y = part // nrep, part % nrep
                                sy = lax.rem(y - mine[3] + nrep, nrep)
                                first = part * PART
                                if part == PIECE // PART - 1:
                                    terms = [
                                        gw_ref[
                                            d * fine : (d + 1) * fine,
                                            j * channels : (j + 1) * channels,
                                        ]
                                        for j in range(4)
                                    ]
                                    value = jnp.concatenate(terms, axis=0)
                                elif first + PART <= rows:
                                    value = total[d * rows + first : d * rows + first + PART, :]
                                else:
                                    left = rows - first
                                    value = jnp.concatenate(
                                        [
                                            total[d * rows + first : d * rows + rows, :],
                                            jnp.zeros((PART - left, channels), F32),
                                        ],
                                        axis=0,
                                    )
                                lead = sx * nrep + sy if half == 0 else sy * nx + sx
                                ref[half, lead, sz] = value.astype(BF16)


def grad_terms(slot, buf, g, gw, sizes):
    slots, channels = buf.shape
    length = slot.shape[1]
    nz, nx, _, nrep = sizes
    shape = (2, nx * nrep, nz, PART, channels)
    return pl.pallas_call(
        functools.partial(grad_kernel, sizes),
        grid=(GRAD_STEPS,),
        out_shape=(jax.ShapeDtypeStruct(shape, BF16), jax.ShapeDtypeStruct(shape, BF16)),
        in_specs=[
            whole(8, length),
            whole(slots, channels),
            pl.BlockSpec(memory_space=pltpu.HBM),
            whole(*gw.shape),
        ],
        out_specs=(whole(*shape), whole(*shape)),
        scratch_shapes=[
            pltpu.VMEM((length, channels), BF16),
            pltpu.VMEM((g.shape[0], channels), F32),
            pltpu.VMEM(g.shape, BF16),
            pltpu.SemaphoreType.DMA((GRAD_STEPS,)),
        ],
        compiler_params=params(32, dimension_semantics=("arbitrary",)),
        cost_estimate=cost(2 * g.shape[0] * length * channels, 12 << 20),
        name="grad_terms",
    )(slot, buf, g, gw)


def add_kernel(plan, *refs):
    count = sum(len(sources) for sources, _ in plan)
    ins, outs = refs[:count], refs[count:]
    at, to = 0, 0
    for sources, parts in plan:
        group = ins[at : at + len(sources)]
        at += len(sources)
        for part in range(parts):
            value = None
            for ref, (lead, per) in zip(group, sources):
                term = ref[lead + part * per : lead + (part + 1) * per].astype(F32)
                value = term if value is None else value + term
            outs[to][...] = value.astype(BF16)
            to += 1


def pair_kernel(count, *refs):
    ins, outs = refs[: 2 * count], refs[2 * count :]
    for side in range(2):
        for half, out in enumerate(outs):
            parts = out.shape[0]
            value = None
            for ref in ins[side * count : (side + 1) * count]:
                term = ref[half * parts : (half + 1) * parts].astype(F32)
                value = term if value is None else value + term
            rows = value.shape[1]
            out[:, side * rows : (side + 1) * rows, :] = value.astype(BF16)


def add_pairs(a, b):
    parts, rows, channels = a[0].shape
    shape = jax.ShapeDtypeStruct((parts // 2, 2 * rows, channels), BF16)
    return pl.pallas_call(
        functools.partial(pair_kernel, len(a)),
        out_shape=(shape,) * 2,
        in_specs=[VMEM_SPEC] * (2 * len(a)),
        out_specs=(VMEM_SPEC,) * 2,
        compiler_params=params(8),
        cost_estimate=cost(1 << 20, 1 << 20),
        name="add_pairs",
    )(*a, *b)


def add_up(terms):
    plan, arrays, shapes = [], [], []
    for sources, lead_rows, parts in terms:
        per = lead_rows // parts
        plan.append((tuple((lead, per) for _, lead in sources), parts))
        arrays += [a for a, _ in sources]
        tail = sources[0][0].shape[1:]
        shapes += [jax.ShapeDtypeStruct((per, *tail), BF16)] * parts
    nbytes = sum(2 * s.size for s in shapes) * 3
    return pl.pallas_call(
        functools.partial(add_kernel, tuple(plan)),
        out_shape=tuple(shapes),
        in_specs=[VMEM_SPEC] * len(arrays),
        out_specs=(VMEM_SPEC,) * len(shapes),
        compiler_params=params(16),
        cost_estimate=cost(nbytes, nbytes),
        name="add_up",
    )(*arrays)


def final_kernel(sizes, *refs):
    _, _, _, nrep = sizes
    ins, (conv_ref, qkv_ref, proj_ref, piece) = refs[:nrep], refs[nrep:]
    me = lax.axis_index("rep")
    rows, channels = conv_ref.shape
    fine = qkv_ref.shape[0]
    for s, ref in enumerate(ins):
        y = lax.rem(me - s + nrep, nrep)
        for half in range(2):
            start = pl.multiple_of((half * nrep + y) * PART, PART)
            piece[pl.ds(start, PART), :] = ref[half * PART : (half + 1) * PART, :].astype(F32)
    conv_ref[...] = piece[:rows, :]
    base = PIECE - PART
    for j in range(3):
        qkv_ref[:, j * channels : (j + 1) * channels] = piece[base + fine * j : base + fine * (j + 1), :]
    proj_ref[...] = piece[base + 3 * fine : base + 4 * fine, :]


def shifted(a, axis, by):
    size = lax.axis_size(axis)
    return lax.ppermute(a, axis, [(i, (i + by) % size) for i in range(size)])


def per_device(features, neighbours, serial, w_conv, w_qkv, w_proj, cotangent):
    feats = features[0]
    length, channels = feats.shape
    slab_count = lax.axis_size(SPACE)
    sizes = tuple(lax.axis_size(a) for a in ("z", "x", "c", "rep"))
    nz, nx, _, nrep = sizes
    capacity = 2 * length // slab_count
    slots = slab_count * capacity
    up = [(i, i + 1) for i in range(slab_count - 1)]
    down = [(j, i) for i, j in up]

    def exchange(buf):
        parts = buf.reshape(slab_count, capacity, -1)
        out = lax.all_to_all(parts, SPACE, split_axis=0, concat_axis=0, tiled=True)
        return out.reshape(slots, -1)

    below = lax.ppermute(feats[length - RIM :], SPACE, up)
    above = lax.ppermute(feats[:RIM], SPACE, down)
    cot_buf, slot, own_t = pack_cot(serial, cotangent[0], feats, slots, capacity)
    nb = jnp.transpose(neighbours, (2, 0, 1))
    g, row_buf = gather_conv(nb, slot, cot_buf, below, own_t, above, feats, w_conv)
    out_buf, dp_buf, gw = patch(exchange(row_buf), w_qkv, w_proj, length)
    keep, send = grad_terms(slot, exchange(dp_buf), g, gw, sizes)

    got = lax.ppermute(send, "c", [(0, 1), (1, 0)])
    flat = lambda a: a.reshape(2 * nx * nrep, nz, PART, channels)
    keep, got = flat(keep), flat(got)
    half = nx * nrep
    parts = add_up([([(keep, 0), (got, 0)], half, nx), ([(keep, half), (got, half)], half, nrep)])
    *parts, out_buf = lax.optimization_barrier((*parts, out_buf))
    a, b = parts[:nx], parts[nx:]
    a_in = [shifted(a[s], "x", s) for s in range(1, nx)]
    b_in = [shifted(b[s], "rep", s) for s in range(1, nrep)]
    out_in = exchange(out_buf)
    output = return_rows(slot, out_in)
    parts = add_up(
        [
            ([(t, 0) for t in [a[0], *a_in]], nrep, nrep),
            ([(t, 0) for t in [b[0], *b_in]], nx, nx),
        ]
    )
    a, b = parts[:nrep], parts[nrep:]
    a_in = [shifted(a[s], "rep", s) for s in range(1, nrep)]
    b_in = [shifted(b[s], "x", s) for s in range(1, nx)]

    def rows_of(t):
        return t.reshape(nz, PART, channels)

    stay, leave = add_pairs([rows_of(t) for t in (a[0], *a_in)], [rows_of(t) for t in (b[0], *b_in)])
    came = lax.ppermute(leave, "z", [(i, i ^ 1) for i in range(nz)])
    ab = add_up([([(stay, 0), (came, 0)], nz // 2, nz // 2)])
    ab_in = [shifted(ab[s], "z", 2 * s) for s in range(1, nz // 2)]
    (own,) = add_up([([(t, 0) for t in [ab[0], *ab_in]], 1, 1)])
    own = own.reshape(2 * PART, channels)
    everyone = [own] + [shifted(own, "rep", s) for s in range(1, nrep)]
    places = slab_count
    g_conv, g_qkv, g_proj = pl.pallas_call(
        functools.partial(final_kernel, sizes),
        out_shape=(
            jax.ShapeDtypeStruct((w_conv.shape[0] // places, channels), F32),
            jax.ShapeDtypeStruct((channels // places, 3 * channels), F32),
            jax.ShapeDtypeStruct((channels // places, channels), F32),
        ),
        in_specs=[VMEM_SPEC] * nrep,
        out_specs=(VMEM_SPEC,) * 3,
        scratch_shapes=[pltpu.VMEM((PIECE, channels), F32)],
        compiler_params=params(8),
        name="final",
    )(*everyone)
    return (output[None], g_conv, g_qkv, g_proj)


def solution(mesh):
    fine = Mesh(mesh.devices.reshape(8, 4, 2, 4), ("z", "x", "c", "rep"))

    return jax.shard_map(
        per_device,
        mesh=fine,
        in_specs=(
            P("rep", SPACE, None),
            P("rep", SPACE, None),
            P("rep", SPACE),
            P(),
            P(),
            P(),
            P("rep", SPACE, None),
        ),
        out_specs=(P("rep", SPACE, None), P(SPACE, None), P(SPACE, None), P(SPACE, None)),
        check_vma=False,
    )
```

```python
import functools

import jax
import jax.numpy as jnp
from jax import lax
from jax.experimental import pallas as pl
from jax.experimental.pallas import tpu as pltpu
from jax.sharding import Mesh
from jax.sharding import PartitionSpec as P


HEADS = 8
RIM = 128
EPSILON = 1e-05
SPACE = ("z", "x", "c")
VACANT = 512.0
OFFSETS_PER_STEP = 3

F32 = jnp.float32
BF16 = jnp.bfloat16


def iota(shape, dim):
    return lax.broadcasted_iota(jnp.int32, shape, dim)


def mm(a, b):
    return jnp.dot(a, b, preferred_element_type=F32)


def mm_nt(a, b):
    return lax.dot_general(a, b, (((1,), (1,)), ((), ())), preferred_element_type=F32)


def mm_tn(a, b):
    return lax.dot_general(a, b, (((0,), (0,)), ((), ())), preferred_element_type=F32)


def one_hot(mask):
    return jnp.where(mask, 1.0, 0.0).astype(BF16)


def turned(a):
    return jnp.transpose(a.astype(F32), (1, 0))


def cost(flops, nbytes):
    return pl.CostEstimate(flops=int(flops), bytes_accessed=int(nbytes), transcendentals=0)


VMEM_SPEC = pl.BlockSpec(memory_space=pltpu.VMEM)


def in_hbm(a):
    return pltpu.with_memory_space_constraint(a, pltpu.HBM)


def params(mebibytes, **more):
    return pltpu.CompilerParams(vmem_limit_bytes=mebibytes << 20, **more)


def slots_of(serial, capacity, owners):
    length = serial.shape[1]
    owner = lax.div(serial, jnp.int32(length))
    member = iota((owners, length), 0) == owner
    before = one_hot(iota((length, length), 0) < iota((length, length), 1))
    earlier = mm(one_hot(member), before)
    place = earlier + (capacity * iota((owners, length), 0)).astype(F32)
    return jnp.sum(jnp.where(member, place, 0.0), axis=0, keepdims=True)


def pack_kernel(capacity, serial_ref, cot_ref, own_ref, buf_ref, slot_ref, own_t_ref):
    length, _ = cot_ref.shape
    slots = buf_ref.shape[0]
    slot = slots_of(serial_ref[...], capacity, slots // capacity)
    slot_ref[...] = jnp.broadcast_to(slot, slot_ref.shape)
    mask = iota((slots, length), 0) == slot.astype(jnp.int32)
    taken = jnp.sum(jnp.where(mask, 1.0, 0.0), axis=1, keepdims=True)
    vacant = jnp.where(taken > 0.5, 0.0, VACANT)
    buf_ref[...] = (mm(one_hot(mask), cot_ref[...]) + vacant).astype(BF16)
    own_t_ref[...] = turned(own_ref[...]).astype(BF16)


def whole(*shape):
    return pl.BlockSpec(shape, lambda i: (0,) * len(shape))


def pack_cot(serial, cot, own, slots, capacity):
    length, channels = cot.shape
    return pl.pallas_call(
        functools.partial(pack_kernel, capacity),
        grid=(1,),
        out_shape=(
            jax.ShapeDtypeStruct((slots, channels), BF16),
            jax.ShapeDtypeStruct((8, length), F32),
            jax.ShapeDtypeStruct((channels, length), BF16),
        ),
        in_specs=[whole(1, length), whole(length, channels), whole(length, channels)],
        out_specs=(whole(slots, channels), whole(8, length), whole(channels, length)),
        compiler_params=params(12),
        cost_estimate=cost(2 * slots * length * channels, 2 << 20),
        name="pack_cot",
    )(in_hbm(serial), in_hbm(cot), in_hbm(own))


def conv_kernel(
    nb_ref,
    slot_ref,
    cot_ref,
    below_ref,
    own_t_ref,
    above_ref,
    own_ref,
    w_ref,
    g_ref,
    buf_ref,
    table,
    held,
    acc,
):
    step = pl.program_id(0)
    last = pl.num_programs(0) - 1
    length, channels = own_ref.shape
    slots = buf_ref.shape[0]
    rows = table.shape[1]
    index = (lax.axis_index("z") * lax.axis_size("x") + lax.axis_index("x")) * lax.axis_size(
        "c"
    ) + lax.axis_index("c")
    base = index * length - RIM

    def gather():
        for j in range(nb_ref.shape[0]):
            linked = nb_ref[j]
            local = jnp.where(linked < 0, -1, linked - base)
            pick = one_hot(iota((rows, length), 0) == local)
            gathered = mm(table[...], pick).astype(BF16)
            g_ref[j * channels : (j + 1) * channels, :] = gathered
            held[j * channels : (j + 1) * channels, :] = gathered

    @pl.when(step == 0)
    def _():
        table[:, :RIM] = turned(below_ref[...]).astype(BF16)
        table[:, RIM : RIM + length] = own_t_ref[...]
        table[:, RIM + length :] = turned(above_ref[...]).astype(BF16)
        acc[...] = jnp.zeros_like(acc)
        gather()

    @pl.when(jnp.logical_and(step > 0, step < last))
    def _():
        acc[...] += mm_tn(w_ref[...], held[...])
        gather()

    @pl.when(step == last)
    def _():
        total = acc[...] + mm_tn(w_ref[...], held[...])
        mixed = (own_ref[...].astype(F32) + turned(total)).astype(BF16)
        pick = one_hot(iota((slots, length), 0) == slot_ref[0:1, :].astype(jnp.int32))
        buf_ref[:, :channels] = mm(pick, mixed).astype(BF16)
        buf_ref[:, channels:] = cot_ref[...]


def gather_conv(nb, slot, cot_buf, below, own_t, above, own, w_conv):
    length, channels = own.shape
    slots = cot_buf.shape[0]
    count = nb.shape[0]
    per = OFFSETS_PER_STEP
    steps = count // per
    rows = length + 2 * RIM
    return pl.pallas_call(
        conv_kernel,
        grid=(steps + 1,),
        out_shape=(
            pltpu.HBM((count * channels, length), BF16),
            jax.ShapeDtypeStruct((slots, 2 * channels), BF16),
        ),
        in_specs=[
            pl.BlockSpec((per, 1, length), lambda i: (jnp.minimum(i, steps - 1), 0, 0)),
            whole(8, length),
            whole(slots, channels),
            whole(RIM, channels),
            whole(channels, length),
            whole(RIM, channels),
            whole(length, channels),
            pl.BlockSpec((per * channels, channels), lambda i: (jnp.maximum(i - 1, 0), 0)),
        ],
        out_specs=(
            pl.BlockSpec((per * channels, length), lambda i: (jnp.minimum(i, steps - 1), 0)),
            whole(slots, 2 * channels),
        ),
        scratch_shapes=[
            pltpu.VMEM((channels, rows), BF16),
            pltpu.VMEM((per * channels, length), BF16),
            pltpu.VMEM((channels, length), F32),
        ],
        compiler_params=params(32, dimension_semantics=("arbitrary",)),
        cost_estimate=cost(2 * count * length * channels * (rows + channels), 12 << 20),
        name="gather_conv",
    )(in_hbm(nb), slot, cot_buf, below, own_t, above, in_hbm(own), in_hbm(w_conv))


def patch_kernel(
    capacity,
    buf_ref,
    wqkv_ref,
    wproj_ref,
    out_ref,
    dp_ref,
    gw_ref,
    key_s,
    value_s,
    query_s,
    datt_s,
    key_t,
    value_t,
    query_t,
    datt_t,
    att_t,
    dq_t,
    dk,
    dv,
):
    slots, channels = dp_ref.shape
    groups, length, group = dk.shape
    depth = channels // HEADS
    factor = depth ** (-0.5)

    mark = buf_ref[:, channels : channels + 128][:, 0:1]
    valid = jnp.broadcast_to(mark.astype(F32), (slots, 128)) < VACANT / 2
    senders = slots // capacity
    lowest = capacity * iota((senders, slots), 0)
    place = iota((senders, slots), 1)
    own = one_hot(jnp.logical_and(place >= lowest, place < lowest + capacity))
    counts = mm(own, one_hot(valid)).astype(BF16)
    earlier = one_hot(capacity * iota((slots, senders), 1) + capacity <= iota((slots, senders), 0))
    within = jnp.bitwise_and(iota((slots, 128), 0), capacity - 1).astype(F32)
    col = jnp.where(valid, mm(earlier, counts) + within, -1.0)
    row = jnp.transpose(col, (1, 0))[0:1, :].astype(jnp.int32)
    rows = mm(one_hot(iota((length, slots), 0) == row), buf_ref[...])
    patched, upstream = rows[:, :channels], rows[:, channels:].astype(BF16)

    values_t = turned(patched)
    centre_t = values_t - jnp.mean(values_t, axis=0, keepdims=True)
    inverse = lax.rsqrt(jnp.mean(centre_t * centre_t, axis=0, keepdims=True) + EPSILON)
    centred_t = centre_t * inverse
    normed_t = centred_t.astype(BF16)
    w_qkv = wqkv_ref[...]
    qkv_t = mm_tn(w_qkv, normed_t)
    d_att = mm_nt(upstream, wproj_ref[...]).astype(BF16)
    query_t[...] = (qkv_t[:channels] * factor).astype(BF16)
    key_t[...] = qkv_t[channels : 2 * channels].astype(BF16)
    value_t[...] = qkv_t[2 * channels :].astype(BF16)
    datt_t[...] = turned(d_att).astype(BF16)
    for source, target in ((query_t, query_s), (key_t, key_s), (value_t, value_s)):
        flat = turned(source[...]).astype(BF16)
        for g in range(groups):
            target[g] = flat[:, g * group : (g + 1) * group]
    for g in range(groups):
        datt_s[g] = d_att[:, g * group : (g + 1) * group]

    lane = iota((length, group), 1)
    zero = jnp.zeros((), BF16)

    def rows_only(a, h):
        parts = [a[h * depth : (h + 1) * depth]]
        if h > 0:
            parts = [jnp.zeros((h * depth, length), BF16), *parts]
        if (h + 1) * depth < group:
            parts = [*parts, jnp.zeros((group - (h + 1) * depth, length), BF16)]
        return jnp.concatenate(parts, axis=0)

    def heads_of(g, carry):
        start = pl.multiple_of(g * group, group)
        k_g, v_g, q_g, da_g = key_s[g], value_s[g], query_s[g], datt_s[g]
        q_tg, da_tg = query_t[pl.ds(start, group), :], datt_t[pl.ds(start, group), :]
        dk_g = jnp.zeros((length, group), F32)
        dv_g = jnp.zeros((length, group), F32)
        for h in range(group // depth):
            in_lanes = jnp.logical_and(lane >= h * depth, lane < (h + 1) * depth)
            at = pl.ds(pl.multiple_of(start + h * depth, depth), depth)
            scores = mm(k_g, rows_only(q_tg, h))
            e = jnp.exp(scores - jnp.max(scores, axis=0, keepdims=True))
            p = e * (1.0 / jnp.sum(e, axis=0, keepdims=True))
            pb = p.astype(BF16)
            attended = mm(value_t[at, :], pb)
            att_t[at, :] = attended
            dv_g = dv_g + mm(pb, jnp.where(in_lanes, da_g, zero))
            dp = mm(v_g, rows_only(da_tg, h))
            row_term = jnp.sum(datt_t[at, :].astype(F32) * attended, axis=0, keepdims=True)
            ds = (p * (dp - row_term)).astype(BF16)
            dq_t[at, :] = mm(key_t[at, :], ds)
            dk_g = dk_g + mm(ds, jnp.where(in_lanes, q_g, zero))
        dk[g] = dk_g
        dv[g] = dv_g
        return carry

    lax.fori_loop(0, groups, heads_of, 0)

    attended_t = att_t[...].astype(BF16)
    out_patch = (patched + mm(turned(attended_t).astype(BF16), wproj_ref[...])).astype(BF16)
    gw_ref[:, 3 * channels :] = mm(attended_t, upstream)
    dq_full = dq_t[...] * factor
    gw_ref[:, :channels] = mm(normed_t, turned(dq_full).astype(BF16))
    d_norm = mm(w_qkv[:, :channels], dq_full.astype(BF16))
    for part, ref in ((1, dk), (2, dv)):
        for g in range(groups):
            at = part * channels + g * group
            grads = ref[g]
            gw_ref[:, at : at + group] = mm(normed_t, grads.astype(BF16))
            d_norm = d_norm + mm(w_qkv[:, at : at + group], turned(grads).astype(BF16))
    d_layer = inverse * (
        d_norm
        - jnp.mean(d_norm, axis=0, keepdims=True)
        - centred_t * jnp.mean(d_norm * centred_t, axis=0, keepdims=True)
    )
    d_patch = (upstream.astype(F32) + turned(d_layer)).astype(BF16)
    key = jnp.broadcast_to(col[:, 0:1].astype(jnp.int32), (slots, length))
    back = one_hot(iota((slots, length), 1) == key)
    dp_ref[...] = mm(back, d_patch).astype(BF16)
    out_ref[...] = mm(back, out_patch).astype(BF16)


def patch(buf, w_qkv, w_proj, length, capacity):
    slots, channels = buf.shape[0], buf.shape[1] // 2
    group = 128
    groups = channels // group
    return pl.pallas_call(
        functools.partial(patch_kernel, capacity),
        out_shape=(
            jax.ShapeDtypeStruct((slots, channels), BF16),
            jax.ShapeDtypeStruct((slots, channels), BF16),
            jax.ShapeDtypeStruct((channels, 4 * channels), F32),
        ),
        in_specs=[VMEM_SPEC] * 3,
        out_specs=(VMEM_SPEC,) * 3,
        scratch_shapes=[pltpu.VMEM((groups, length, group), BF16)] * 4
        + [pltpu.VMEM((channels, length), BF16)] * 4
        + [pltpu.VMEM((channels, length), F32)] * 2
        + [pltpu.VMEM((groups, length, group), F32)] * 2,
        compiler_params=params(32),
        cost_estimate=cost(14e9, 4 << 20),
        name="patch",
    )(buf, w_qkv, w_proj)


def unpack(slot, buf):
    slots = buf.shape[0]
    length = slot.shape[1]
    wide = jnp.transpose(jnp.broadcast_to(slot[0:1, :], (128, length)), (1, 0))
    key = jnp.broadcast_to(wide[:, 0:1].astype(jnp.int32), (length, slots))
    return mm(one_hot(iota((length, slots), 1) == key), buf).astype(BF16)


def output_kernel(slot_ref, buf_ref, out_ref):
    out_ref[...] = unpack(slot_ref[...], buf_ref[...])


def return_rows(slot, buf):
    length, channels = slot.shape[1], buf.shape[1]
    return pl.pallas_call(
        output_kernel,
        out_shape=jax.ShapeDtypeStruct((length, channels), BF16),
        in_specs=[VMEM_SPEC] * 2,
        out_specs=VMEM_SPEC,
        compiler_params=params(12),
        cost_estimate=cost(2 * length * buf.shape[0] * channels, 1 << 20),
        name="return_rows",
    )(slot, buf)


GRAD_STEPS = 9
PIECE = 128
PART = 16


def grad_kernel(
    sizes, slot_ref, buf_ref, g_ref, gw_ref, keep_ref, send_ref, d_mixed, total, near, sems
):
    step = pl.program_id(0)
    nz, nx, nc, nrep = sizes
    block = g_ref.shape[0] // GRAD_STEPS
    channels = buf_ref.shape[1]

    def fetch(i):
        at = pl.ds(pl.multiple_of(i * block, block), block)
        return pltpu.make_async_copy(g_ref.at[at, :], near.at[at, :], sems.at[i])

    @pl.when(step == 0)
    def _():
        for i in range(GRAD_STEPS):
            fetch(i).start()
        d_mixed[...] = unpack(slot_ref[...], buf_ref[...])

    fetch(step).wait()
    at = pl.ds(pl.multiple_of(step * block, block), block)
    total[at, :] = mm(near[at, :], d_mixed[...])

    @pl.when(step == pl.num_programs(0) - 1)
    def _():
        mine = (lax.axis_index("z"), lax.axis_index("x"), lax.axis_index("c"), lax.axis_index("rep"))
        rows = total.shape[0] // (nz * nx * nc)
        fine = gw_ref.shape[0] // (nz * nx * nc)
        sxs = [lax.rem(x - mine[1] + nx, nx) for x in range(nx)]
        sys = [lax.rem(y - mine[3] + nrep, nrep) for y in range(nrep)]
        leads = [
            [[sx * nrep + sy for sy in sys] for sx in sxs],
            [[sy * nx + sx for sy in sys] for sx in sxs],
        ]
        for core in range(nc):
            for is_mine, ref in ((True, keep_ref), (False, send_ref)):
                same = mine[2] == core

                @pl.when(same if is_mine else jnp.logical_not(same))
                def _(core=core, ref=ref):
                    for z in range(nz):
                        pair = lax.rem(z % 2 + lax.rem(mine[0], 2), 2)
                        four = lax.rem(z // 2 - lax.div(mine[0], 2) + nz // 2, nz // 2)
                        sz = pair * (nz // 2) + four
                        for x in range(nx):
                            d = (z * nx + x) * nc + core
                            for part in range(PIECE // PART):
                                half, y = part // nrep, part % nrep
                                first = part * PART
                                if part == PIECE // PART - 1:
                                    terms = [
                                        gw_ref[
                                            d * fine : (d + 1) * fine,
                                            j * channels : (j + 1) * channels,
                                        ]
                                        for j in range(4)
                                    ]
                                    value = jnp.concatenate(terms, axis=0)
                                elif first + PART <= rows:
                                    value = total[d * rows + first : d * rows + first + PART, :]
                                else:
                                    left = rows - first
                                    value = jnp.concatenate(
                                        [
                                            total[d * rows + first : d * rows + rows, :],
                                            jnp.zeros((PART - left, channels), F32),
                                        ],
                                        axis=0,
                                    )
                                ref[half, leads[half][x][y], sz] = value.astype(BF16)


def grad_terms(slot, buf, g, gw, sizes):
    slots, channels = buf.shape
    length = slot.shape[1]
    nz, nx, _, nrep = sizes
    shape = (2, nx * nrep, nz, PART, channels)
    return pl.pallas_call(
        functools.partial(grad_kernel, sizes),
        grid=(GRAD_STEPS,),
        out_shape=(jax.ShapeDtypeStruct(shape, BF16), jax.ShapeDtypeStruct(shape, BF16)),
        in_specs=[
            whole(8, length),
            whole(slots, channels),
            pl.BlockSpec(memory_space=pltpu.HBM),
            whole(*gw.shape),
        ],
        out_specs=(whole(*shape), whole(*shape)),
        scratch_shapes=[
            pltpu.VMEM((length, channels), BF16),
            pltpu.VMEM((g.shape[0], channels), F32),
            pltpu.VMEM(g.shape, BF16),
            pltpu.SemaphoreType.DMA((GRAD_STEPS,)),
        ],
        compiler_params=params(32, dimension_semantics=("arbitrary",)),
        cost_estimate=cost(2 * g.shape[0] * length * channels, 12 << 20),
        name="grad_terms",
    )(slot, buf, g, gw)


def add_kernel(plan, *refs):
    count = sum(len(sources) for sources, _ in plan)
    ins, outs = refs[:count], refs[count:]
    at, to = 0, 0
    for sources, parts in plan:
        group = ins[at : at + len(sources)]
        at += len(sources)
        for part in range(parts):
            value = None
            for ref, (lead, per) in zip(group, sources):
                term = ref[lead + part * per : lead + (part + 1) * per].astype(F32)
                value = term if value is None else value + term
            outs[to][...] = value.astype(BF16)
            to += 1


def pair_kernel(count, *refs):
    ins, outs = refs[: 2 * count], refs[2 * count :]
    for side in range(2):
        for half, out in enumerate(outs):
            parts = out.shape[0]
            value = None
            for ref in ins[side * count : (side + 1) * count]:
                term = ref[half * parts : (half + 1) * parts].astype(F32)
                value = term if value is None else value + term
            rows = value.shape[1]
            out[:, side * rows : (side + 1) * rows, :] = value.astype(BF16)


def add_pairs(a, b):
    parts, rows, channels = a[0].shape
    shape = jax.ShapeDtypeStruct((parts // 2, 2 * rows, channels), BF16)
    return pl.pallas_call(
        functools.partial(pair_kernel, len(a)),
        out_shape=(shape,) * 2,
        in_specs=[VMEM_SPEC] * (2 * len(a)),
        out_specs=(VMEM_SPEC,) * 2,
        compiler_params=params(8),
        cost_estimate=cost(1 << 20, 1 << 20),
        name="add_pairs",
    )(*a, *b)


def add_up(terms):
    plan, arrays, shapes = [], [], []
    for sources, lead_rows, parts in terms:
        per = lead_rows // parts
        plan.append((tuple((lead, per) for _, lead in sources), parts))
        arrays += [a for a, _ in sources]
        tail = sources[0][0].shape[1:]
        shapes += [jax.ShapeDtypeStruct((per, *tail), BF16)] * parts
    nbytes = sum(2 * s.size for s in shapes) * 3
    return pl.pallas_call(
        functools.partial(add_kernel, tuple(plan)),
        out_shape=tuple(shapes),
        in_specs=[VMEM_SPEC] * len(arrays),
        out_specs=(VMEM_SPEC,) * len(shapes),
        compiler_params=params(16),
        cost_estimate=cost(nbytes, nbytes),
        name="add_up",
    )(*arrays)


def final_kernel(sizes, *refs):
    _, _, _, nrep = sizes
    ins, (conv_ref, qkv_ref, proj_ref, piece) = refs[:nrep], refs[nrep:]
    me = lax.axis_index("rep")
    rows, channels = conv_ref.shape
    fine = qkv_ref.shape[0]
    for s, ref in enumerate(ins):
        y = lax.rem(me - s + nrep, nrep)
        for half in range(2):
            start = pl.multiple_of((half * nrep + y) * PART, PART)
            piece[pl.ds(start, PART), :] = ref[half * PART : (half + 1) * PART, :].astype(F32)
    conv_ref[...] = piece[:rows, :]
    base = PIECE - PART
    for j in range(3):
        qkv_ref[:, j * channels : (j + 1) * channels] = piece[base + fine * j : base + fine * (j + 1), :]
    proj_ref[...] = piece[base + 3 * fine : base + 4 * fine, :]


def shifted(a, axis, by):
    size = lax.axis_size(axis)
    return lax.ppermute(a, axis, [(i, (i + by) % size) for i in range(size)])


def per_device(features, neighbours, serial, w_conv, w_qkv, w_proj, cotangent):
    feats = features[0]
    length, channels = feats.shape
    slab_count = lax.axis_size(SPACE)
    sizes = tuple(lax.axis_size(a) for a in ("z", "x", "c", "rep"))
    nz, nx, _, nrep = sizes
    capacity = 2 * length // slab_count
    slots = slab_count * capacity
    up = [(i, i + 1) for i in range(slab_count - 1)]
    down = [(j, i) for i, j in up]

    def exchange(buf):
        parts = buf.reshape(slab_count, capacity, -1)
        out = lax.all_to_all(parts, SPACE, split_axis=0, concat_axis=0, tiled=True)
        return out.reshape(slots, -1)

    below = lax.ppermute(feats[length - RIM :], SPACE, up)
    above = lax.ppermute(feats[:RIM], SPACE, down)
    cot_buf, slot, own_t = pack_cot(serial, cotangent[0], feats, slots, capacity)
    nb = jnp.transpose(neighbours, (2, 0, 1))
    g, row_buf = gather_conv(nb, slot, cot_buf, below, own_t, above, feats, w_conv)
    out_buf, dp_buf, gw = patch(exchange(row_buf), w_qkv, w_proj, length, capacity)
    keep, send = grad_terms(slot, exchange(dp_buf), g, gw, sizes)

    got = lax.ppermute(send, "c", [(0, 1), (1, 0)])
    flat = lambda a: a.reshape(2 * nx * nrep, nz, PART, channels)
    keep, got = flat(keep), flat(got)
    half = nx * nrep
    parts = add_up([([(keep, 0), (got, 0)], half, nx), ([(keep, half), (got, half)], half, nrep)])
    *parts, out_buf = lax.optimization_barrier((*parts, out_buf))
    a, b = parts[:nx], parts[nx:]
    a_in = [shifted(a[s], "x", s) for s in range(1, nx)]
    b_in = [shifted(b[s], "rep", s) for s in range(1, nrep)]
    out_in = exchange(out_buf)
    output = return_rows(slot, out_in)
    parts = add_up(
        [
            ([(t, 0) for t in [a[0], *a_in]], nrep, nrep),
            ([(t, 0) for t in [b[0], *b_in]], nx, nx),
        ]
    )
    a, b = parts[:nrep], parts[nrep:]
    a_in = [shifted(a[s], "rep", s) for s in range(1, nrep)]
    b_in = [shifted(b[s], "x", s) for s in range(1, nx)]

    def rows_of(t):
        return t.reshape(nz, PART, channels)

    stay, leave = add_pairs([rows_of(t) for t in (a[0], *a_in)], [rows_of(t) for t in (b[0], *b_in)])
    came = lax.ppermute(leave, "z", [(i, i ^ 1) for i in range(nz)])
    ab = add_up([([(stay, 0), (came, 0)], nz // 2, nz // 2)])
    ab_in = [shifted(ab[s], "z", 2 * s) for s in range(1, nz // 2)]
    (own,) = add_up([([(t, 0) for t in [ab[0], *ab_in]], 1, 1)])
    own = own.reshape(2 * PART, channels)
    everyone = [own] + [shifted(own, "rep", s) for s in range(1, nrep)]
    places = slab_count
    g_conv, g_qkv, g_proj = pl.pallas_call(
        functools.partial(final_kernel, sizes),
        out_shape=(
            jax.ShapeDtypeStruct((w_conv.shape[0] // places, channels), F32),
            jax.ShapeDtypeStruct((channels // places, 3 * channels), F32),
            jax.ShapeDtypeStruct((channels // places, channels), F32),
        ),
        in_specs=[VMEM_SPEC] * nrep,
        out_specs=(VMEM_SPEC,) * 3,
        scratch_shapes=[pltpu.VMEM((PIECE, channels), F32)],
        compiler_params=params(8),
        name="final",
    )(*everyone)
    return (output[None], g_conv, g_qkv, g_proj)


def solution(mesh):
    fine = Mesh(mesh.devices.reshape(8, 4, 2, 4), ("z", "x", "c", "rep"))

    return jax.shard_map(
        per_device,
        mesh=fine,
        in_specs=(
            P("rep", SPACE, None),
            P("rep", SPACE, None),
            P("rep", SPACE),
            P(),
            P(),
            P(),
            P("rep", SPACE, None),
        ),
        out_specs=(P("rep", SPACE, None), P(SPACE, None), P(SPACE, None), P(SPACE, None)),
        check_vma=False,
    )
```

```python
import functools

import jax
import jax.numpy as jnp
from jax import lax
from jax.experimental import pallas as pl
from jax.experimental.pallas import tpu as pltpu
from jax.sharding import Mesh
from jax.sharding import PartitionSpec as P


HEADS = 8
RIM = 128
EPSILON = 1e-05
SPACE = ("z", "x", "c")
VACANT = 512.0
OFFSETS_PER_STEP = 3

F32 = jnp.float32
BF16 = jnp.bfloat16


def iota(shape, dim):
    return lax.broadcasted_iota(jnp.int32, shape, dim)


def mm(a, b):
    return jnp.dot(a, b, preferred_element_type=F32)


def mm_nt(a, b):
    return lax.dot_general(a, b, (((1,), (1,)), ((), ())), preferred_element_type=F32)


def mm_tn(a, b):
    return lax.dot_general(a, b, (((0,), (0,)), ((), ())), preferred_element_type=F32)


def one_hot(mask):
    return jnp.where(mask, 1.0, 0.0).astype(BF16)


def turned(a):
    return jnp.transpose(a.astype(F32), (1, 0))


def cost(flops, nbytes):
    return pl.CostEstimate(flops=int(flops), bytes_accessed=int(nbytes), transcendentals=0)


VMEM_SPEC = pl.BlockSpec(memory_space=pltpu.VMEM)


def in_hbm(a):
    return pltpu.with_memory_space_constraint(a, pltpu.HBM)


def params(mebibytes, **more):
    return pltpu.CompilerParams(vmem_limit_bytes=mebibytes << 20, **more)


def slots_of(serial, capacity, owners):
    length = serial.shape[1]
    owner = lax.div(serial, jnp.int32(length))
    member = iota((owners, length), 0) == owner
    before = one_hot(iota((length, length), 0) < iota((length, length), 1))
    earlier = mm(one_hot(member), before)
    place = earlier + (capacity * iota((owners, length), 0)).astype(F32)
    return jnp.sum(jnp.where(member, place, 0.0), axis=0, keepdims=True)


def pack_kernel(capacity, serial_ref, cot_ref, own_ref, buf_ref, slot_ref, own_t_ref):
    length, _ = cot_ref.shape
    slots = buf_ref.shape[0]
    slot = slots_of(serial_ref[...], capacity, slots // capacity)
    slot_ref[...] = jnp.broadcast_to(slot, slot_ref.shape)
    mask = iota((slots, length), 0) == slot.astype(jnp.int32)
    taken = jnp.sum(jnp.where(mask, 1.0, 0.0), axis=1, keepdims=True)
    vacant = jnp.where(taken > 0.5, 0.0, VACANT)
    buf_ref[...] = (mm(one_hot(mask), cot_ref[...]) + vacant).astype(BF16)
    own_t_ref[...] = turned(own_ref[...]).astype(BF16)


def whole(*shape):
    return pl.BlockSpec(shape, lambda i: (0,) * len(shape))


def pack_cot(serial, cot, own, slots, capacity):
    length, channels = cot.shape
    return pl.pallas_call(
        functools.partial(pack_kernel, capacity),
        grid=(1,),
        out_shape=(
            jax.ShapeDtypeStruct((slots, channels), BF16),
            jax.ShapeDtypeStruct((8, length), F32),
            jax.ShapeDtypeStruct((channels, length), BF16),
        ),
        in_specs=[whole(1, length), whole(length, channels), whole(length, channels)],
        out_specs=(whole(slots, channels), whole(8, length), whole(channels, length)),
        compiler_params=params(12),
        cost_estimate=cost(2 * slots * length * channels, 2 << 20),
        name="pack_cot",
    )(in_hbm(serial), in_hbm(cot), in_hbm(own))


def conv_kernel(
    nb_ref,
    slot_ref,
    cot_ref,
    below_ref,
    own_t_ref,
    above_ref,
    own_ref,
    w_ref,
    g_ref,
    buf_ref,
    table,
    held,
    acc,
):
    step = pl.program_id(0)
    last = pl.num_programs(0) - 1
    length, channels = own_ref.shape
    slots = buf_ref.shape[0]
    rows = table.shape[1]
    index = (lax.axis_index("z") * lax.axis_size("x") + lax.axis_index("x")) * lax.axis_size(
        "c"
    ) + lax.axis_index("c")
    base = index * length - RIM

    def gather():
        for j in range(nb_ref.shape[0]):
            linked = nb_ref[j]
            local = jnp.where(linked < 0, -1, linked - base)
            pick = one_hot(iota((rows, length), 0) == local)
            gathered = mm(table[...], pick).astype(BF16)
            g_ref[j * channels : (j + 1) * channels, :] = gathered
            held[j * channels : (j + 1) * channels, :] = gathered

    @pl.when(step == 0)
    def _():
        table[:, :RIM] = turned(below_ref[...]).astype(BF16)
        table[:, RIM : RIM + length] = own_t_ref[...]
        table[:, RIM + length :] = turned(above_ref[...]).astype(BF16)
        acc[...] = jnp.zeros_like(acc)
        gather()

    @pl.when(jnp.logical_and(step > 0, step < last))
    def _():
        acc[...] += mm_tn(w_ref[...], held[...])
        gather()

    @pl.when(step == last)
    def _():
        total = acc[...] + mm_tn(w_ref[...], held[...])
        mixed = (own_ref[...].astype(F32) + turned(total)).astype(BF16)
        pick = one_hot(iota((slots, length), 0) == slot_ref[0:1, :].astype(jnp.int32))
        buf_ref[:, :channels] = mm(pick, mixed).astype(BF16)
        buf_ref[:, channels:] = cot_ref[...]


def gather_conv(nb, slot, cot_buf, below, own_t, above, own, w_conv):
    length, channels = own.shape
    slots = cot_buf.shape[0]
    count = nb.shape[0]
    per = OFFSETS_PER_STEP
    steps = count // per
    rows = length + 2 * RIM
    return pl.pallas_call(
        conv_kernel,
        grid=(steps + 1,),
        out_shape=(
            pltpu.HBM((count * channels, length), BF16),
            jax.ShapeDtypeStruct((slots, 2 * channels), BF16),
        ),
        in_specs=[
            pl.BlockSpec((per, 1, length), lambda i: (jnp.minimum(i, steps - 1), 0, 0)),
            whole(8, length),
            whole(slots, channels),
            whole(RIM, channels),
            whole(channels, length),
            whole(RIM, channels),
            whole(length, channels),
            pl.BlockSpec((per * channels, channels), lambda i: (jnp.maximum(i - 1, 0), 0)),
        ],
        out_specs=(
            pl.BlockSpec((per * channels, length), lambda i: (jnp.minimum(i, steps - 1), 0)),
            whole(slots, 2 * channels),
        ),
        scratch_shapes=[
            pltpu.VMEM((channels, rows), BF16),
            pltpu.VMEM((per * channels, length), BF16),
            pltpu.VMEM((channels, length), F32),
        ],
        compiler_params=params(32, dimension_semantics=("arbitrary",)),
        cost_estimate=cost(2 * count * length * channels * (rows + channels), 12 << 20),
        name="gather_conv",
    )(in_hbm(nb), slot, cot_buf, below, own_t, above, in_hbm(own), in_hbm(w_conv))


def patch_kernel(
    capacity,
    buf_ref,
    wqkv_ref,
    wproj_ref,
    out_ref,
    dp_ref,
    gw_ref,
    key_s,
    value_s,
    query_s,
    datt_s,
    key_t,
    value_t,
    query_t,
    datt_t,
    att_t,
    dq_t,
    dk,
    dv,
):
    slots, channels = dp_ref.shape
    groups, length, group = dk.shape
    depth = channels // HEADS
    factor = depth ** (-0.5)

    mark = buf_ref[:, channels : channels + 128][:, 0:1]
    valid = jnp.broadcast_to(mark.astype(F32), (slots, 128)) < VACANT / 2
    senders = slots // capacity
    lowest = capacity * iota((senders, slots), 0)
    place = iota((senders, slots), 1)
    own = one_hot(jnp.logical_and(place >= lowest, place < lowest + capacity))
    counts = mm(own, one_hot(valid)).astype(BF16)
    earlier = one_hot(capacity * iota((slots, senders), 1) + capacity <= iota((slots, senders), 0))
    within = jnp.bitwise_and(iota((slots, 128), 0), capacity - 1).astype(F32)
    col = jnp.where(valid, mm(earlier, counts) + within, -1.0)
    row = jnp.transpose(col, (1, 0))[0:1, :].astype(jnp.int32)
    rows = mm(one_hot(iota((length, slots), 0) == row), buf_ref[...])
    patched, upstream = rows[:, :channels], rows[:, channels:].astype(BF16)

    values_t = turned(patched)
    centre_t = values_t - jnp.mean(values_t, axis=0, keepdims=True)
    inverse = lax.rsqrt(jnp.mean(centre_t * centre_t, axis=0, keepdims=True) + EPSILON)
    centred_t = centre_t * inverse
    normed_t = centred_t.astype(BF16)
    w_qkv = wqkv_ref[...]
    qkv_t = mm_tn(w_qkv, normed_t)
    d_att = mm_nt(upstream, wproj_ref[...]).astype(BF16)
    query_t[...] = (qkv_t[:channels] * factor).astype(BF16)
    key_t[...] = qkv_t[channels : 2 * channels].astype(BF16)
    value_t[...] = qkv_t[2 * channels :].astype(BF16)
    datt_t[...] = turned(d_att).astype(BF16)
    for source, target in ((query_t, query_s), (key_t, key_s), (value_t, value_s)):
        flat = turned(source[...]).astype(BF16)
        for g in range(groups):
            target[g] = flat[:, g * group : (g + 1) * group]
    for g in range(groups):
        datt_s[g] = d_att[:, g * group : (g + 1) * group]

    lane = iota((length, group), 1)
    zero = jnp.zeros((), BF16)

    def rows_only(a, h):
        parts = [a[h * depth : (h + 1) * depth]]
        if h > 0:
            parts = [jnp.zeros((h * depth, length), BF16), *parts]
        if (h + 1) * depth < group:
            parts = [*parts, jnp.zeros((group - (h + 1) * depth, length), BF16)]
        return jnp.concatenate(parts, axis=0)

    def heads_of(g, carry):
        start = pl.multiple_of(g * group, group)
        k_g, v_g, q_g, da_g = key_s[g], value_s[g], query_s[g], datt_s[g]
        q_tg, da_tg = query_t[pl.ds(start, group), :], datt_t[pl.ds(start, group), :]
        dk_g = jnp.zeros((length, group), F32)
        dv_g = jnp.zeros((length, group), F32)
        for h in range(group // depth):
            in_lanes = jnp.logical_and(lane >= h * depth, lane < (h + 1) * depth)
            at = pl.ds(pl.multiple_of(start + h * depth, depth), depth)
            scores = mm(k_g, rows_only(q_tg, h))
            e = jnp.exp(scores - jnp.max(scores, axis=0, keepdims=True))
            p = e * (1.0 / jnp.sum(e, axis=0, keepdims=True))
            pb = p.astype(BF16)
            attended = mm(value_t[at, :], pb)
            att_t[at, :] = attended
            dv_g = dv_g + mm(pb, jnp.where(in_lanes, da_g, zero))
            dp = mm(v_g, rows_only(da_tg, h))
            row_term = jnp.sum(datt_t[at, :].astype(F32) * attended, axis=0, keepdims=True)
            ds = (p * (dp - row_term)).astype(BF16)
            dq_t[at, :] = mm(key_t[at, :], ds)
            dk_g = dk_g + mm(ds, jnp.where(in_lanes, q_g, zero))
        dk[g] = dk_g
        dv[g] = dv_g
        return carry

    lax.fori_loop(0, groups, heads_of, 0)

    attended_t = att_t[...].astype(BF16)
    out_patch = (patched + mm(turned(attended_t).astype(BF16), wproj_ref[...])).astype(BF16)
    gw_ref[:, 3 * channels :] = mm(attended_t, upstream)
    dq_full = dq_t[...] * factor
    gw_ref[:, :channels] = mm(normed_t, turned(dq_full).astype(BF16))
    d_norm = mm(w_qkv[:, :channels], dq_full.astype(BF16))
    for part, ref in ((1, dk), (2, dv)):
        for g in range(groups):
            at = part * channels + g * group
            grads = ref[g]
            gw_ref[:, at : at + group] = mm(normed_t, grads.astype(BF16))
            d_norm = d_norm + mm(w_qkv[:, at : at + group], turned(grads).astype(BF16))
    d_layer = inverse * (
        d_norm
        - jnp.mean(d_norm, axis=0, keepdims=True)
        - centred_t * jnp.mean(d_norm * centred_t, axis=0, keepdims=True)
    )
    d_patch = (upstream.astype(F32) + turned(d_layer)).astype(BF16)
    key = jnp.broadcast_to(col[:, 0:1].astype(jnp.int32), (slots, length))
    back = one_hot(iota((slots, length), 1) == key)
    dp_ref[...] = mm(back, d_patch).astype(BF16)
    out_ref[...] = mm(back, out_patch).astype(BF16)


def patch(buf, w_qkv, w_proj, length, capacity):
    slots, channels = buf.shape[0], buf.shape[1] // 2
    group = 128
    groups = channels // group
    return pl.pallas_call(
        functools.partial(patch_kernel, capacity),
        out_shape=(
            jax.ShapeDtypeStruct((slots, channels), BF16),
            jax.ShapeDtypeStruct((slots, channels), BF16),
            jax.ShapeDtypeStruct((channels, 4 * channels), F32),
        ),
        in_specs=[VMEM_SPEC] * 3,
        out_specs=(VMEM_SPEC,) * 3,
        scratch_shapes=[pltpu.VMEM((groups, length, group), BF16)] * 4
        + [pltpu.VMEM((channels, length), BF16)] * 4
        + [pltpu.VMEM((channels, length), F32)] * 2
        + [pltpu.VMEM((groups, length, group), F32)] * 2,
        compiler_params=params(32),
        cost_estimate=cost(14e9, 4 << 20),
        name="patch",
    )(buf, w_qkv, w_proj)


def unpack(slot, buf):
    slots = buf.shape[0]
    length = slot.shape[1]
    wide = jnp.transpose(jnp.broadcast_to(slot[0:1, :], (128, length)), (1, 0))
    key = jnp.broadcast_to(wide[:, 0:1].astype(jnp.int32), (length, slots))
    return mm(one_hot(iota((length, slots), 1) == key), buf).astype(BF16)


def output_kernel(slot_ref, buf_ref, out_ref):
    out_ref[...] = unpack(slot_ref[...], buf_ref[...])


def return_rows(slot, buf):
    length, channels = slot.shape[1], buf.shape[1]
    return pl.pallas_call(
        output_kernel,
        out_shape=jax.ShapeDtypeStruct((length, channels), BF16),
        in_specs=[VMEM_SPEC] * 2,
        out_specs=VMEM_SPEC,
        compiler_params=params(12),
        cost_estimate=cost(2 * length * buf.shape[0] * channels, 1 << 20),
        name="return_rows",
    )(slot, buf)


GRAD_STEPS = 3
PIECE = 128
PART = 16


def grad_kernel(
    sizes, slot_ref, buf_ref, g_ref, gw_ref, keep_ref, send_ref, d_mixed, total
):
    step = pl.program_id(0)
    nz, nx, nc, nrep = sizes
    block = g_ref.shape[0] // GRAD_STEPS
    channels = buf_ref.shape[1]

    @pl.when(step == 0)
    def _():
        d_mixed[...] = unpack(slot_ref[...], buf_ref[...])

    at = pl.ds(pl.multiple_of(step * block, block), block)
    total[at, :] = mm(g_ref[at, :], d_mixed[...])

    @pl.when(step == pl.num_programs(0) - 1)
    def _():
        mine = (lax.axis_index("z"), lax.axis_index("x"), lax.axis_index("c"), lax.axis_index("rep"))
        rows = total.shape[0] // (nz * nx * nc)
        fine = gw_ref.shape[0] // (nz * nx * nc)
        sxs = [lax.rem(x - mine[1] + nx, nx) for x in range(nx)]
        sys = [lax.rem(y - mine[3] + nrep, nrep) for y in range(nrep)]
        leads = [
            [[sx * nrep + sy for sy in sys] for sx in sxs],
            [[sy * nx + sx for sy in sys] for sx in sxs],
        ]
        for core in range(nc):
            for is_mine, ref in ((True, keep_ref), (False, send_ref)):
                same = mine[2] == core

                @pl.when(same if is_mine else jnp.logical_not(same))
                def _(core=core, ref=ref):
                    for z in range(nz):
                        pair = lax.rem(z % 2 + lax.rem(mine[0], 2), 2)
                        four = lax.rem(z // 2 - lax.div(mine[0], 2) + nz // 2, nz // 2)
                        sz = pair * (nz // 2) + four
                        for x in range(nx):
                            d = (z * nx + x) * nc + core
                            for part in range(PIECE // PART):
                                half, y = part // nrep, part % nrep
                                first = part * PART
                                if part == PIECE // PART - 1:
                                    terms = [
                                        gw_ref[
                                            d * fine : (d + 1) * fine,
                                            j * channels : (j + 1) * channels,
                                        ]
                                        for j in range(4)
                                    ]
                                    value = jnp.concatenate(terms, axis=0)
                                elif first + PART <= rows:
                                    value = total[d * rows + first : d * rows + first + PART, :]
                                else:
                                    left = rows - first
                                    value = jnp.concatenate(
                                        [
                                            total[d * rows + first : d * rows + rows, :],
                                            jnp.zeros((PART - left, channels), F32),
                                        ],
                                        axis=0,
                                    )
                                ref[half, leads[half][x][y], sz] = value.astype(BF16)


def grad_terms(slot, buf, g, gw, sizes):
    slots, channels = buf.shape
    length = slot.shape[1]
    nz, nx, _, nrep = sizes
    shape = (2, nx * nrep, nz, PART, channels)
    return pl.pallas_call(
        functools.partial(grad_kernel, sizes),
        grid=(GRAD_STEPS,),
        out_shape=(jax.ShapeDtypeStruct(shape, BF16), jax.ShapeDtypeStruct(shape, BF16)),
        in_specs=[
            whole(8, length),
            whole(slots, channels),
            VMEM_SPEC,
            whole(*gw.shape),
        ],
        out_specs=(whole(*shape), whole(*shape)),
        scratch_shapes=[
            pltpu.VMEM((length, channels), BF16),
            pltpu.VMEM((g.shape[0], channels), F32),
        ],
        compiler_params=params(32, dimension_semantics=("arbitrary",)),
        cost_estimate=cost(2 * g.shape[0] * length * channels, 12 << 20),
        name="grad_terms",
    )(slot, buf, g, gw)


def add_kernel(plan, *refs):
    count = sum(len(sources) for sources, _ in plan)
    ins, outs = refs[:count], refs[count:]
    at, to = 0, 0
    for sources, parts in plan:
        group = ins[at : at + len(sources)]
        at += len(sources)
        for part in range(parts):
            value = None
            for ref, (lead, per) in zip(group, sources):
                term = ref[lead + part * per : lead + (part + 1) * per].astype(F32)
                value = term if value is None else value + term
            outs[to][...] = value.astype(BF16)
            to += 1


def pair_kernel(count, *refs):
    ins, outs = refs[: 2 * count], refs[2 * count :]
    for side in range(2):
        for half, out in enumerate(outs):
            parts = out.shape[0]
            value = None
            for ref in ins[side * count : (side + 1) * count]:
                term = ref[half * parts : (half + 1) * parts].astype(F32)
                value = term if value is None else value + term
            rows = value.shape[1]
            out[:, side * rows : (side + 1) * rows, :] = value.astype(BF16)


def add_pairs(a, b):
    parts, rows, channels = a[0].shape
    shape = jax.ShapeDtypeStruct((parts // 2, 2 * rows, channels), BF16)
    return pl.pallas_call(
        functools.partial(pair_kernel, len(a)),
        out_shape=(shape,) * 2,
        in_specs=[VMEM_SPEC] * (2 * len(a)),
        out_specs=(VMEM_SPEC,) * 2,
        compiler_params=params(8),
        cost_estimate=cost(1 << 20, 1 << 20),
        name="add_pairs",
    )(*a, *b)


def add_up(terms):
    plan, arrays, shapes = [], [], []
    for sources, lead_rows, parts in terms:
        per = lead_rows // parts
        plan.append((tuple((lead, per) for _, lead in sources), parts))
        arrays += [a for a, _ in sources]
        tail = sources[0][0].shape[1:]
        shapes += [jax.ShapeDtypeStruct((per, *tail), BF16)] * parts
    nbytes = sum(2 * s.size for s in shapes) * 3
    return pl.pallas_call(
        functools.partial(add_kernel, tuple(plan)),
        out_shape=tuple(shapes),
        in_specs=[VMEM_SPEC] * len(arrays),
        out_specs=(VMEM_SPEC,) * len(shapes),
        compiler_params=params(16),
        cost_estimate=cost(nbytes, nbytes),
        name="add_up",
    )(*arrays)


def final_kernel(sizes, *refs):
    _, _, _, nrep = sizes
    ins, (conv_ref, qkv_ref, proj_ref, piece) = refs[:nrep], refs[nrep:]
    me = lax.axis_index("rep")
    rows, channels = conv_ref.shape
    fine = qkv_ref.shape[0]
    for s, ref in enumerate(ins):
        y = lax.rem(me - s + nrep, nrep)
        for half in range(2):
            start = pl.multiple_of((half * nrep + y) * PART, PART)
            piece[pl.ds(start, PART), :] = ref[half * PART : (half + 1) * PART, :].astype(F32)
    conv_ref[...] = piece[:rows, :]
    base = PIECE - PART
    for j in range(3):
        qkv_ref[:, j * channels : (j + 1) * channels] = piece[base + fine * j : base + fine * (j + 1), :]
    proj_ref[...] = piece[base + 3 * fine : base + 4 * fine, :]


def shifted(a, axis, by):
    size = lax.axis_size(axis)
    return lax.ppermute(a, axis, [(i, (i + by) % size) for i in range(size)])


def per_device(features, neighbours, serial, w_conv, w_qkv, w_proj, cotangent):
    feats = features[0]
    length, channels = feats.shape
    slab_count = lax.axis_size(SPACE)
    sizes = tuple(lax.axis_size(a) for a in ("z", "x", "c", "rep"))
    nz, nx, _, nrep = sizes
    capacity = 2 * length // slab_count
    slots = slab_count * capacity
    up = [(i, i + 1) for i in range(slab_count - 1)]
    down = [(j, i) for i, j in up]

    def exchange(buf):
        parts = buf.reshape(slab_count, capacity, -1)
        out = lax.all_to_all(parts, SPACE, split_axis=0, concat_axis=0, tiled=True)
        return out.reshape(slots, -1)

    below = lax.ppermute(feats[length - RIM :], SPACE, up)
    above = lax.ppermute(feats[:RIM], SPACE, down)
    cot_buf, slot, own_t = pack_cot(serial, cotangent[0], feats, slots, capacity)
    nb = jnp.transpose(neighbours, (2, 0, 1))
    g, row_buf = gather_conv(nb, slot, cot_buf, below, own_t, above, feats, w_conv)
    out_buf, dp_buf, gw = patch(exchange(row_buf), w_qkv, w_proj, length, capacity)
    keep, send = grad_terms(slot, exchange(dp_buf), g, gw, sizes)

    got = lax.ppermute(send, "c", [(0, 1), (1, 0)])
    flat = lambda a: a.reshape(2 * nx * nrep, nz, PART, channels)
    keep, got = flat(keep), flat(got)
    half = nx * nrep
    parts = add_up([([(keep, 0), (got, 0)], half, nx), ([(keep, half), (got, half)], half, nrep)])
    *parts, out_buf = lax.optimization_barrier((*parts, out_buf))
    a, b = parts[:nx], parts[nx:]
    a_in = [shifted(a[s], "x", s) for s in range(1, nx)]
    b_in = [shifted(b[s], "rep", s) for s in range(1, nrep)]
    out_in = exchange(out_buf)
    output = return_rows(slot, out_in)
    parts = add_up(
        [
            ([(t, 0) for t in [a[0], *a_in]], nrep, nrep),
            ([(t, 0) for t in [b[0], *b_in]], nx, nx),
        ]
    )
    a, b = parts[:nrep], parts[nrep:]
    a_in = [shifted(a[s], "rep", s) for s in range(1, nrep)]
    b_in = [shifted(b[s], "x", s) for s in range(1, nx)]

    def rows_of(t):
        return t.reshape(nz, PART, channels)

    stay, leave = add_pairs([rows_of(t) for t in (a[0], *a_in)], [rows_of(t) for t in (b[0], *b_in)])
    came = lax.ppermute(leave, "z", [(i, i ^ 1) for i in range(nz)])
    ab = add_up([([(stay, 0), (came, 0)], nz // 2, nz // 2)])
    ab_in = [shifted(ab[s], "z", 2 * s) for s in range(1, nz // 2)]
    (own,) = add_up([([(t, 0) for t in [ab[0], *ab_in]], 1, 1)])
    own = own.reshape(2 * PART, channels)
    everyone = [own] + [shifted(own, "rep", s) for s in range(1, nrep)]
    places = slab_count
    g_conv, g_qkv, g_proj = pl.pallas_call(
        functools.partial(final_kernel, sizes),
        out_shape=(
            jax.ShapeDtypeStruct((w_conv.shape[0] // places, channels), F32),
            jax.ShapeDtypeStruct((channels // places, 3 * channels), F32),
            jax.ShapeDtypeStruct((channels // places, channels), F32),
        ),
        in_specs=[VMEM_SPEC] * nrep,
        out_specs=(VMEM_SPEC,) * 3,
        scratch_shapes=[pltpu.VMEM((PIECE, channels), F32)],
        compiler_params=params(8),
        name="final",
    )(*everyone)
    return (output[None], g_conv, g_qkv, g_proj)


def solution(mesh):
    fine = Mesh(mesh.devices.reshape(8, 4, 2, 4), ("z", "x", "c", "rep"))

    return jax.shard_map(
        per_device,
        mesh=fine,
        in_specs=(
            P("rep", SPACE, None),
            P("rep", SPACE, None),
            P("rep", SPACE),
            P(),
            P(),
            P(),
            P("rep", SPACE, None),
        ),
        out_specs=(P("rep", SPACE, None), P(SPACE, None), P(SPACE, None), P(SPACE, None)),
        check_vma=False,
    )
```
